32 devices in a mesh: gx: 2 (over x), gy: 4 (over z), gz: 4 (over y, core).
Axes of the slice: x: 2, y: 2, z: 4, core: 2. Of those that a mesh axis runs over, the one named last changes fastest.
Arguments:
- positions: float32 [3, 4, 8, 16, 128], P(None, 'gx', 'gy', 'gz'), may hold values from 0 to 11
- velocities: float32 [3, 4, 8, 16, 128], P(None, 'gx', 'gy', 'gz'), may hold values from -0.6 to 0.6
- counts: int32 [4, 8, 16], P('gx', 'gy', 'gz'), may hold values from 96 to 128
Outputs:
- new_velocity: float32 [3, 4, 8, 16, 128], P(None, 'gx', 'gy', 'gz')
- moved: float32 [3, 4, 8, 16, 128], P(None, 'gx', 'gy', 'gz')
The draws below stay inside these ranges and needn't reach their ends.
All inputs are finite; a program needn't handle non-finite values.
Results may differ from the reference program's by a relative error of at most 0.0003.
Values sent between devices are 32-bit elements; how exact they have to be, the bound alone decides.
No kernel may reach another device: no remote copies, remote signals or barrier semaphores. Data moves between devices by JAX's collectives and lax.ppermute only.
A program may use at most 64 MiB of HBM per device.

```python
import jax
import jax.numpy as jnp
from jax import lax

SLOTS = 128
STEPS = 1
NX = 4
NY = 8
NZ = 16


def set_ends(result, key, low, largest):
    place = [jax.random.randint(jax.random.fold_in(key, axis), (), 0, length) for axis, length in enumerate(result.shape)]
    longest = result.shape.index(max(result.shape))
    next_to = place[:longest] + [(place[longest] + 1) % result.shape[longest]] + place[longest + 1:]
    return result.at[tuple(place)].set(low).at[tuple(next_to)].set(largest)


def steps_of(stream_key, shape, split, least, high):
    def one(axis_at, parts):
        heights = jax.random.uniform(jax.random.fold_in(jax.random.fold_in(stream_key, 6), axis_at), (parts,), jnp.float32, least / len(split), high / len(split))
        return jnp.repeat(jnp.exp(heights), shape[axis_at] // parts).reshape((-1,) + (1,) * (len(shape) - axis_at - 1))

    loudness = one(*split[0])
    for cut in split[1:]:
        loudness = loudness * one(*cut)
    return loudness


def gaussian(stream_key, dims, width, bound, cuts=(), kind=jnp.bfloat16):
    entries = width * jax.random.normal(stream_key, dims, jnp.float32)
    if cuts:
        entries = entries * steps_of(stream_key, dims, cuts, -0.22, 0.18)
    return jnp.clip(entries, -bound, bound).astype(kind)


def setup_inputs(seed: int = 0) -> dict:
    seeds = jax.random.split(jax.random.key(seed), 4)
    positions = jnp.clip(11.0 * jax.random.uniform(seeds[0], (3, NX, NY, NZ, SLOTS), jnp.float32) ** steps_of(seeds[0], (3, NX, NY, NZ, SLOTS), ((1, 2), (2, 4), (3, 4)), -0.2, 0.2), 0.0, 11.0)
    velocities = gaussian(seeds[1], (3, NX, NY, NZ, SLOTS), 0.1, 0.6, ((1, 2), (2, 4), (3, 4)), jnp.float32)
    counts = set_ends(jax.random.randint(seeds[2], (NX, NY, NZ), SLOTS - SLOTS // 4, SLOTS + 1), jax.random.fold_in(seeds[2], 1), SLOTS - SLOTS // 4, SLOTS).astype(jnp.int32)
    return {"positions": positions, "velocities": velocities, "counts": counts}


CELL_EDGE = 11.0
CUT_SQ = 25.0
WIDTH_DENSITY = 4.0
WIDTH_PAIR = 2.0
SCALE_DENSITY = 0.4
SCALE_PAIR = 0.3
DENSITY_REF = 1.0
TIME_STEP = 0.5
BOX_PAIRS = (
    ((0, 0, 0), (1, 0, 0)), ((0, 0, 0), (0, 1, 0)), ((0, 0, 0), (0, 0, 1)),
    ((0, 0, 0), (1, 1, 0)), ((0, 0, 0), (1, 0, 1)), ((0, 0, 0), (0, 1, 1)),
    ((0, 0, 0), (1, 1, 1)), ((0, 1, 0), (1, 0, 0)), ((0, 0, 1), (1, 0, 0)),
    ((0, 0, 1), (0, 1, 0)), ((0, 1, 0), (1, 0, 1)), ((0, 0, 1), (1, 1, 0)),
    ((1, 0, 0), (0, 1, 1)),
)


def smooth_parts(radius_sq):
    inside = radius_sq < CUT_SQ
    remain = 1.0 - radius_sq / CUT_SQ
    smooth = jnp.where(inside, remain * remain, 0.0)
    smooth_slope = jnp.where(inside, -2.0 * remain / CUT_SQ, 0.0)
    return smooth, smooth_slope


def separation_of(slab_a, slab_b, offset):
    shift_vec = jnp.array(offset, jnp.float32) * CELL_EDGE
    return slab_b[:, :, None, :] - slab_a[:, :, :, None] + shift_vec[:, None, None, None]


def tile_weight(mask_a, mask_b, self_tile):
    weight = mask_a[:, :, None] * mask_b[:, None, :]
    if self_tile:
        weight = weight * (1.0 - jnp.eye(mask_a.shape[1], dtype=mask_a.dtype))
    return weight


def pair_density(slab_a, slab_b, mask_a, mask_b, offset, self_tile):
    separation = separation_of(slab_a, slab_b, offset)
    radius_sq = jnp.sum(separation * separation, axis=0)
    smooth, unused_slope = smooth_parts(radius_sq)
    pair_term = tile_weight(mask_a, mask_b, self_tile) * SCALE_DENSITY * jnp.exp(-radius_sq / WIDTH_DENSITY) * smooth
    return jnp.sum(pair_term, axis=2), jnp.sum(pair_term, axis=1)


def pair_force(slab_a, slab_b, mask_a, mask_b, grad_a, grad_b, offset, self_tile):
    separation = separation_of(slab_a, slab_b, offset)
    radius_sq = jnp.sum(separation * separation, axis=0)
    smooth, smooth_slope = smooth_parts(radius_sq)
    density_fall = SCALE_DENSITY * jnp.exp(-radius_sq / WIDTH_DENSITY)
    density_slope = density_fall * (smooth_slope - smooth / WIDTH_DENSITY)
    pair_fall = SCALE_PAIR * jnp.exp(-radius_sq / WIDTH_PAIR)
    pair_slope = pair_fall * (smooth_slope - smooth / WIDTH_PAIR)
    factor = tile_weight(mask_a, mask_b, self_tile) * 2.0 * (
        pair_slope + (grad_a[:, :, None] + grad_b[:, None, :]) * density_slope)
    pushed = factor[None] * separation
    return jnp.sum(pushed, axis=3), -jnp.sum(pushed, axis=2)


def pick_block(cell_count, most):
    for candidate in range(most, 0, -1):
        if cell_count % candidate == 0:
            return candidate
    return 1


def take_cells(field, first_cell, block_size, axis_index):
    return lax.dynamic_slice_in_dim(field, first_cell, block_size, axis_index)


def density_sweep(slab_a, slab_b, mask_a, mask_b, offset, self_tile, most):
    cell_count, slot_count = mask_a.shape
    block_size = pick_block(cell_count, most)
    empty_sums = jnp.zeros((cell_count, slot_count), mask_a.dtype)

    def visit_block(block_index, running):
        row_sums, col_sums = running
        first_cell = (block_index * block_size).astype(jnp.int32)
        row_block, col_block = pair_density(
            take_cells(slab_a, first_cell, block_size, 1), take_cells(slab_b, first_cell, block_size, 1),
            take_cells(mask_a, first_cell, block_size, 0), take_cells(mask_b, first_cell, block_size, 0),
            offset, self_tile)
        row_sums = lax.dynamic_update_slice_in_dim(row_sums, row_block, first_cell, 0)
        col_sums = lax.dynamic_update_slice_in_dim(col_sums, col_block, first_cell, 0)
        return row_sums, col_sums

    return lax.fori_loop(0, cell_count // block_size, visit_block, (empty_sums, empty_sums))


def force_sweep(slab_a, slab_b, mask_a, mask_b, grad_a, grad_b, offset, self_tile, most):
    cell_count, slot_count = mask_a.shape
    block_size = pick_block(cell_count, most)
    empty_push = jnp.zeros((3, cell_count, slot_count), mask_a.dtype)

    def visit_block(block_index, running):
        push_a, push_b = running
        first_cell = (block_index * block_size).astype(jnp.int32)
        block_a, block_b = pair_force(
            take_cells(slab_a, first_cell, block_size, 1), take_cells(slab_b, first_cell, block_size, 1),
            take_cells(mask_a, first_cell, block_size, 0), take_cells(mask_b, first_cell, block_size, 0),
            take_cells(grad_a, first_cell, block_size, 0), take_cells(grad_b, first_cell, block_size, 0),
            offset, self_tile)
        push_a = lax.dynamic_update_slice_in_dim(push_a, block_a, first_cell, 1)
        push_b = lax.dynamic_update_slice_in_dim(push_b, block_b, first_cell, 1)
        return push_a, push_b

    return lax.fori_loop(0, cell_count // block_size, visit_block, (empty_push, empty_push))


def moved_cells(field, corner):
    return jnp.roll(field, shift=(-corner[0], -corner[1], -corner[2]), axis=(-4, -3, -2))


def restore_cells(field, corner):
    return jnp.roll(field, shift=(corner[0], corner[1], corner[2]), axis=(-4, -3, -2))


def total_forces(positions, live):
    grid_shape = live.shape
    cell_count = grid_shape[0] * grid_shape[1] * grid_shape[2]
    slot_count = grid_shape[3]
    flat_pos = positions.reshape(3, cell_count, slot_count)
    flat_live = live.reshape(cell_count, slot_count)
    row_block, unused_cols = density_sweep(flat_pos, flat_pos, flat_live, flat_live, (0, 0, 0), True, 64)
    density = row_block.reshape(grid_shape)
    for corner_a, corner_b in BOX_PAIRS:
        offset = (corner_b[0] - corner_a[0], corner_b[1] - corner_a[1], corner_b[2] - corner_a[2])
        pos_a = moved_cells(positions, corner_a).reshape(3, cell_count, slot_count)
        pos_b = moved_cells(positions, corner_b).reshape(3, cell_count, slot_count)
        live_a = moved_cells(live, corner_a).reshape(cell_count, slot_count)
        live_b = moved_cells(live, corner_b).reshape(cell_count, slot_count)
        row_block, col_block = density_sweep(pos_a, pos_b, live_a, live_b, offset, False, 64)
        density = density + restore_cells(row_block.reshape(grid_shape), corner_a)
        density = density + restore_cells(col_block.reshape(grid_shape), corner_b)
    embed_grad = live * 2.0 * (density - DENSITY_REF)
    flat_grad = embed_grad.reshape(cell_count, slot_count)
    push_a, unused_push = force_sweep(flat_pos, flat_pos, flat_live, flat_live, flat_grad, flat_grad, (0, 0, 0), True, 64)
    forces = push_a.reshape(positions.shape)
    for corner_a, corner_b in BOX_PAIRS:
        offset = (corner_b[0] - corner_a[0], corner_b[1] - corner_a[1], corner_b[2] - corner_a[2])
        pos_a = moved_cells(positions, corner_a).reshape(3, cell_count, slot_count)
        pos_b = moved_cells(positions, corner_b).reshape(3, cell_count, slot_count)
        live_a = moved_cells(live, corner_a).reshape(cell_count, slot_count)
        live_b = moved_cells(live, corner_b).reshape(cell_count, slot_count)
        grad_a = moved_cells(embed_grad, corner_a).reshape(cell_count, slot_count)
        grad_b = moved_cells(embed_grad, corner_b).reshape(cell_count, slot_count)
        push_a, push_b = force_sweep(pos_a, pos_b, live_a, live_b, grad_a, grad_b, offset, False, 64)
        forces = forces + restore_cells(push_a.reshape(positions.shape), corner_a)
        forces = forces + restore_cells(push_b.reshape(positions.shape), corner_b)
    return forces


def live_slots(counts, slot_count):
    slot_index = lax.broadcasted_iota(jnp.int32, counts.shape + (slot_count,), 3)
    return (slot_index < counts[..., None].astype(jnp.int32)).astype(jnp.float32)


def reference(positions, velocities, counts):
    live = live_slots(counts, positions.shape[4])
    running_position = positions
    running_velocity = velocities
    for moment in range(STEPS):
        forces = total_forces(running_position, live)
        running_velocity = running_velocity + TIME_STEP * forces
        running_position = running_position + TIME_STEP * running_velocity
    return running_velocity * live[None], (running_position - positions) * live[None]
```

```python
import math
import jax
import jax.numpy as jnp
import numpy as np
from jax import lax
from jax.experimental import pallas as pl
from jax.experimental.pallas import tpu as pltpu
from jax.sharding import PartitionSpec as P

CELL_EDGE = 11.0
HALF_EDGE = 5.5
CUT_SQ = 25.0
WIDTH_DENSITY = 4.0
WIDTH_PAIR = 2.0
SCALE_DENSITY = 0.4
SCALE_PAIR = 0.3
DENSITY_REF = 1.0
TIME_STEP = 0.5
FAR = 4096.0
AXES = ("gx", "gy", "gz")

TOP_E = CUT_SQ / WIDTH_DENSITY
TOP = TOP_E / math.log(2.0)
SPREAD = math.sqrt(TOP / CUT_SQ)
DENSITY_SCALE = SCALE_DENSITY * math.exp(-TOP_E) / TOP**2
PAIR_SHIFT = 4.0 * TOP / CUT_SQ
DENSITY_SHIFT = 8.0 * TOP / CUT_SQ
FORCE_SCALE = -SCALE_PAIR * math.exp(-2.0 * TOP_E) / TOP**2
GRAD_SCALE = SCALE_DENSITY / (2.0 * SCALE_PAIR) * math.exp(TOP_E)

ROWS = 144
TERMS = 32
LEFT_PARTS = (0, 0, 1, 0, 2, 1)
RIGHT_PARTS = (0, 1, 0, 2, 0, 1)
ONE_ROW = 18
NORM_ROW = 21


def neighbour_layers(field, axis, name):
    count = lax.axis_size(name)
    size = field.shape[axis]
    first = lax.slice_in_dim(field, 0, 1, axis=axis)
    last = lax.slice_in_dim(field, size - 1, size, axis=axis)
    if count == 1:
        return last, first
    if count == 2:
        swapped = lax.ppermute(jnp.concatenate([last, first], axis=axis), name, [(0, 1), (1, 0)])
        return lax.slice_in_dim(swapped, 0, 1, axis=axis), lax.slice_in_dim(swapped, 1, 2, axis=axis)
    below = lax.ppermute(last, name, [(d, (d + 1) % count) for d in range(count)])
    above = lax.ppermute(first, name, [(d, (d - 1) % count) for d in range(count)])
    return below, above


def with_halo(field):
    for axis, name in ((1, "gx"), (2, "gy"), (3, "gz")):
        below, above = neighbour_layers(field, axis, name)
        field = jnp.concatenate([below, field, above], axis=axis)
    return field


def split_three(value):
    high = value.astype(jnp.bfloat16).astype(jnp.float32)
    rest = value - high
    middle = rest.astype(jnp.bfloat16).astype(jnp.float32)
    return high, middle, rest - middle


def rows_of(contract_a, contract_b, a, b):
    return lax.dot_general(
        a, b, (((contract_a,), (contract_b,)), ((), ())), preferred_element_type=jnp.float32
    )


def left_matrix():
    pick = np.zeros((TERMS, TERMS), np.float32)
    for comp in range(3):
        where_part = {0: 6 * comp, 1: 6 * comp + 1, 2: 6 * comp + 3}
        for term, part in enumerate(LEFT_PARTS):
            pick[where_part[part], 6 * comp + term] = 0.5
    for term in range(3):
        pick[NORM_ROW + term, ONE_ROW + term] = 1.0
        pick[ONE_ROW, NORM_ROW + term] = 1.0
    return pick


def block_step(extent, slots):
    inner_x, inner_y, inner_z = extent
    ext_y, ext_z = inner_y + 2, inner_z + 2
    cells = (inner_x + 2) * ext_y * ext_z
    vert_x, vert_y, vert_z = inner_x + 1, inner_y + 1, inner_z + 1
    verts = vert_x * vert_y * vert_z
    rows8 = verts * 8
    spare = (cells * slots) // ROWS
    lanes = 8 * slots

    def cell_of(cx, cy, cz):
        return (cx * ext_y + cy) * ext_z + cz

    def vert_of(vx, vy, vz):
        return (vx * vert_y + vy) * vert_z + vz

    def kernel(ext_ref, pos_ref, vel_ref, live_ref, pick_ref, vel_out, moved_out,
               corner, dest, terms, right, left, left_t, grad_row, dens_lane, grad_lane, spare_vert, spare_count):
        for vx in range(vert_x):
            for vy in range(vert_y):
                for vz in range(vert_z):
                    v = vert_of(vx, vy, vz)
                    for kxy in range(4):
                        c = cell_of(vx + kxy // 2, vy + kxy % 2, vz)
                        for comp in range(3):
                            corner[comp, v * 8 + 2 * kxy : v * 8 + 2 * kxy + 2, :] = ext_ref[comp, c : c + 2, :]
        row_id = lax.broadcasted_iota(jnp.int32, (rows8, slots), 0)
        near = None
        for comp in range(3):
            upper = ((row_id >> (2 - comp)) & 1) == 1
            x = corner[comp]
            low = x < HALF_EDGE
            test = jnp.where(upper, jnp.where(low, 1.0, 0.0), jnp.where(low | (x > 0.5 * FAR), 0.0, 1.0))
            near = test if near is None else near * test
        near_b = near.astype(jnp.bfloat16)
        lane_a = lax.broadcasted_iota(jnp.int32, (slots, slots), 0)
        lane_b = lax.broadcasted_iota(jnp.int32, (slots, slots), 1)
        before = jnp.where(lane_a < lane_b, 1.0, 0.0).astype(jnp.bfloat16)
        prefix = jnp.dot(near_b, before, preferred_element_type=jnp.float32)
        total = jnp.dot(near_b, jnp.ones((slots, slots), jnp.bfloat16), preferred_element_type=jnp.float32)
        wide_a = lax.broadcasted_iota(jnp.int32, (rows8, rows8), 0)
        wide_b = lax.broadcasted_iota(jnp.int32, (rows8, rows8), 1)
        earlier = jnp.where((wide_a >> 3 == wide_b >> 3) & (wide_b < wide_a), 1.0, 0.0).astype(jnp.bfloat16)
        offset = jnp.dot(earlier, total.astype(jnp.bfloat16), preferred_element_type=jnp.float32)
        dest[...] = jnp.where(near > 0.5, prefix + offset, -1.0)
        most = jnp.max(offset + total)

        norm = 0.5 * TOP
        one = jnp.ones((rows8, slots), jnp.float32)
        values = []
        for comp in range(3):
            upper = ((row_id >> (2 - comp)) & 1) == 1
            x = (corner[comp] - jnp.where(upper, 0.0, CELL_EDGE)) * SPREAD
            norm = norm - x * x
            parts = split_three(2.0 * x)
            values += [parts[part] for part in RIGHT_PARTS]
        values += [one] * 3 + list(split_three(norm))
        values += [jnp.zeros((rows8, slots), jnp.float32)] * (TERMS - len(values))
        for term in range(TERMS):
            terms[pl.ds(term, rows8, stride=TERMS), :] = values[term]

        def pack(v, carry):
            for k in range(8):
                start = pl.multiple_of((v * 8 + k) * TERMS, TERMS)
                right[v, :, k * slots : (k + 1) * slots] = terms[pl.ds(start, TERMS), :].astype(jnp.bfloat16)
            return carry

        lax.fori_loop(0, verts, pack, 0)
        dens_lane[...] = jnp.zeros(dens_lane.shape, jnp.float32)

        def list_and_density(v, first_row, slot):
            start = pl.multiple_of(v * 8, 8)
            place = dest[pl.ds(start, 8), :] - first_row
            row = lax.broadcasted_iota(jnp.int32, (ROWS, slots), 0).astype(jnp.float32)
            chosen = jnp.concatenate(
                [jnp.where(row == place[k : k + 1, :], 1.0, 0.0).astype(jnp.bfloat16) for k in range(8)], axis=1
            )
            near_right = right[v]
            listed = rows_of(1, 1, chosen, near_right).astype(jnp.bfloat16)
            left_t[slot] = rows_of(1, 1, near_right, chosen).astype(jnp.bfloat16)
            lefts = jnp.dot(listed, pick_ref[...], preferred_element_type=jnp.float32).astype(jnp.bfloat16)
            left[slot] = lefts
            vz = v % vert_z
            vy = (v // vert_z) % vert_y
            vx = v // (vert_z * vert_y)
            sums = None
            for k in range(8):
                s = jnp.dot(lefts, right[v, :, k * slots : (k + 1) * slots], preferred_element_type=jnp.float32)
                s = jnp.maximum(s, 0.0)
                part = jnp.exp2(s) * (s * s)
                sums = part if sums is None else sums + part
                c = cell_of(vx + (k >> 2), vy + ((k >> 1) & 1), vz + (k & 1))
                dens_lane[c] += jnp.sum(part.reshape(ROWS // 8, 8, slots), axis=0)
            density = jnp.sum(sums, axis=1, keepdims=True) * DENSITY_SCALE
            grad = (2.0 * GRAD_SCALE) * (density - (SCALE_DENSITY + DENSITY_REF))
            grad_row[slot] = jnp.broadcast_to(grad, (ROWS, slots))

        def visit(v, carry):
            list_and_density(v, 0.0, v)
            return carry

        lax.fori_loop(0, verts, visit, 0)
        spare_count[0] = 0

        @pl.when(most > ROWS)
        def _():
            def visit_spare(v, carry):
                def chunk(t, inner):
                    listed = dest[pl.ds(pl.multiple_of(v * 8, 8), 8), :]

                    @pl.when(jnp.max(listed) >= (t * ROWS).astype(jnp.float32))
                    def _():
                        slot = spare_count[0]
                        spare_vert[slot] = v
                        spare_count[0] = slot + 1
                        list_and_density(v, (t * ROWS).astype(jnp.float32), verts + slot)

                    return inner

                return lax.fori_loop(1, (lanes + ROWS - 1) // ROWS, chunk, carry)

            lax.fori_loop(0, verts, visit_spare, 0)

        def finish_density(c, carry):
            density = jnp.sum(dens_lane[c], axis=0, keepdims=True) * DENSITY_SCALE
            grad = (2.0 * GRAD_SCALE) * (density - (SCALE_DENSITY + DENSITY_REF))
            grad_lane[c] = jnp.broadcast_to(grad, (8, slots))
            return carry

        lax.fori_loop(0, cells, finish_density, 0)

        def force_sums(v, k, slot, c):
            s = jnp.dot(left[slot], right[v, :, k * slots : (k + 1) * slots], preferred_element_type=jnp.float32)
            s = jnp.maximum(s, 0.0)
            fall = jnp.exp2(s)
            grads = grad_row[slot] + grad_lane[c, 0:1, :]
            push = (fall * s) * (fall * (s + PAIR_SHIFT) + grads * (s + DENSITY_SHIFT))
            high = push.astype(jnp.bfloat16)
            low = (push - high.astype(jnp.float32)).astype(jnp.bfloat16)
            lt = left_t[slot]
            return rows_of(1, 0, lt, high) + rows_of(1, 0, lt, low)

        def shares(sums, k):
            weight = sums[ONE_ROW : ONE_ROW + 1, :]
            out = []
            for comp in range(3):
                base = 6 * comp
                moment = sums[base : base + 1, :] + sums[base + 1 : base + 2, :] + sums[base + 3 : base + 4, :]
                moment = moment * (0.5 / SPREAD)
                if not (k >> (2 - comp)) & 1:
                    moment = moment + CELL_EDGE * weight
                out.append(moment)
            return out + [weight]

        totals = dens_lane

        def visit_cell(n, carry):
            iz = n % inner_z
            iy = (n // inner_z) % inner_y
            ix = n // (inner_z * inner_y)
            c = cell_of(ix + 1, iy + 1, iz + 1)
            gathered = None
            for k in range(8):
                v = vert_of(ix + 1 - (k >> 2), iy + 1 - ((k >> 1) & 1), iz + 1 - (k & 1))
                part = shares(force_sums(v, k, v, c), k)
                gathered = part if gathered is None else [a + b for a, b in zip(gathered, part)]
            totals[c] = jnp.concatenate(gathered + [jnp.zeros((4, slots), jnp.float32)], axis=0)
            return carry

        lax.fori_loop(0, inner_x * inner_y * inner_z, visit_cell, 0)

        def spare_force(e, carry):
            v = spare_vert[e]
            vz = v % vert_z
            vy = (v // vert_z) % vert_y
            vx = v // (vert_z * vert_y)
            for k in range(8):
                cx, cy, cz = vx + (k >> 2), vy + ((k >> 1) & 1), vz + (k & 1)
                own = (
                    (cx >= 1) & (cx <= inner_x) & (cy >= 1) & (cy <= inner_y) & (cz >= 1) & (cz <= inner_z)
                )

                @pl.when(own)
                def _():
                    c = cell_of(cx, cy, cz)
                    part = shares(force_sums(v, k, verts + e, c), k)
                    totals[c] += jnp.concatenate(part + [jnp.zeros((4, slots), jnp.float32)], axis=0)

            return carry

        lax.fori_loop(0, spare_count[0], spare_force, 0)

        for ix in range(inner_x):
            for iy in range(inner_y):
                c = cell_of(ix + 1, iy + 1, 1)
                n = (ix * inner_y + iy) * inner_z
                for iz in range(inner_z):
                    alive = live_ref[n + iz : n + iz + 1, :]
                    both = totals[c + iz]
                    for comp in range(3):
                        x = pos_ref[comp, n + iz : n + iz + 1, :]
                        force = FORCE_SCALE * (both[comp : comp + 1, :] - x * both[3:4, :])
                        velocity = vel_ref[comp, n + iz : n + iz + 1, :] + TIME_STEP * force
                        velocity = jnp.where(alive > 0.5, velocity, 0.0)
                        vel_out[comp, n + iz : n + iz + 1, :] = velocity
                        moved_out[comp, n + iz : n + iz + 1, :] = TIME_STEP * velocity

    own_cells = inner_x * inner_y * inner_z
    vmem = pl.BlockSpec(memory_space=pltpu.VMEM)
    pairs = verts * 8 * ROWS * slots
    return pl.pallas_call(
        kernel,
        out_shape=(jax.ShapeDtypeStruct((3, own_cells, slots), jnp.float32),) * 2,
        in_specs=[vmem] * 5,
        out_specs=(vmem, vmem),
        scratch_shapes=[
            pltpu.VMEM((3, rows8, slots), jnp.float32),
            pltpu.VMEM((rows8, slots), jnp.float32),
            pltpu.VMEM((rows8 * TERMS, slots), jnp.float32),
            pltpu.VMEM((verts, TERMS, lanes), jnp.bfloat16),
            pltpu.VMEM((verts + spare, ROWS, TERMS), jnp.bfloat16),
            pltpu.VMEM((verts + spare, TERMS, ROWS), jnp.bfloat16),
            pltpu.VMEM((verts + spare, ROWS, slots), jnp.float32),
            pltpu.VMEM((cells, 8, slots), jnp.float32),
            pltpu.VMEM((cells, 8, slots), jnp.float32),
            pltpu.SMEM((spare,), jnp.int32),
            pltpu.SMEM((1,), jnp.int32),
        ],
        compiler_params=pltpu.CompilerParams(vmem_limit_bytes=60 * 2**20),
        cost_estimate=pl.CostEstimate(flops=40 * pairs, bytes_accessed=4 * 3 * cells * slots, transcendentals=2 * pairs),
        name="block_step",
    )


def body(positions, velocities, counts):
    comps, size_x, size_y, size_z, slots = positions.shape
    own_cells = size_x * size_y * size_z
    slot_index = lax.broadcasted_iota(jnp.int32, counts.shape + (slots,), 3)
    live = slot_index < counts[..., None]
    shown = jnp.where(live[None], positions, FAR)
    ext = with_halo(shown)
    step = block_step((size_x, size_y, size_z), slots)
    velocity, moved = step(
        ext.reshape(comps, -1, slots),
        positions.reshape(comps, own_cells, slots),
        velocities.reshape(comps, own_cells, slots),
        live.astype(jnp.float32).reshape(own_cells, slots),
        jnp.asarray(left_matrix(), jnp.bfloat16),
    )
    return velocity.reshape(positions.shape), moved.reshape(positions.shape)


def solution(mesh):
    spec = P(None, *AXES, None)
    return jax.shard_map(
        body,
        mesh=mesh,
        in_specs=(spec, spec, P(*AXES)),
        out_specs=(spec, spec),
        check_vma=False,
    )
```

```python
import math
import jax
import jax.numpy as jnp
import numpy as np
from jax import lax
from jax.experimental import pallas as pl
from jax.experimental.pallas import tpu as pltpu
from jax.sharding import PartitionSpec as P

CELL_EDGE = 11.0
HALF_EDGE = 5.5
CUT_SQ = 25.0
WIDTH_DENSITY = 4.0
WIDTH_PAIR = 2.0
SCALE_DENSITY = 0.4
SCALE_PAIR = 0.3
DENSITY_REF = 1.0
TIME_STEP = 0.5
FAR = 4096.0
AXES = ("gx", "gy", "gz")

TOP_E = CUT_SQ / WIDTH_DENSITY
TOP = TOP_E / math.log(2.0)
SPREAD = math.sqrt(TOP / CUT_SQ)
DENSITY_SCALE = SCALE_DENSITY * math.exp(-TOP_E) / TOP**2
PAIR_SHIFT = 4.0 * TOP / CUT_SQ
DENSITY_SHIFT = 8.0 * TOP / CUT_SQ
FORCE_SCALE = -SCALE_PAIR * math.exp(-2.0 * TOP_E) / TOP**2
GRAD_SCALE = SCALE_DENSITY / (2.0 * SCALE_PAIR) * math.exp(TOP_E)

ROWS = 144
SPARE_ROWS = 32
LEFT_PARTS = (0, 0, 1, 0, 2, 1)
RIGHT_PARTS = (0, 1, 0, 2, 0, 1)
BLOCK = 8
TERMS = 6 * BLOCK
KEPT = 4 * BLOCK
NORM_AT = 3
ONE_AT = 4


def neighbour_layers(field, axis, name):
    count = lax.axis_size(name)
    size = field.shape[axis]
    first = lax.slice_in_dim(field, 0, 1, axis=axis)
    last = lax.slice_in_dim(field, size - 1, size, axis=axis)
    if count == 1:
        return last, first
    if count == 2:
        swapped = lax.ppermute(jnp.concatenate([last, first], axis=axis), name, [(0, 1), (1, 0)])
        return lax.slice_in_dim(swapped, 0, 1, axis=axis), lax.slice_in_dim(swapped, 1, 2, axis=axis)
    below = lax.ppermute(last, name, [(d, (d + 1) % count) for d in range(count)])
    above = lax.ppermute(first, name, [(d, (d - 1) % count) for d in range(count)])
    return below, above


def with_halo(field):
    for axis, name in enumerate(AXES):
        below, above = neighbour_layers(field, axis, name)
        field = jnp.concatenate([below, field, above], axis=axis)
    return field


def split_three(value):
    high = value.astype(jnp.bfloat16).astype(jnp.float32)
    rest = value - high
    middle = rest.astype(jnp.bfloat16).astype(jnp.float32)
    return high, middle, rest - middle


def rows_of(contract_a, contract_b, a, b):
    return lax.dot_general(
        a, b, (((contract_a,), (contract_b,)), ((), ())), preferred_element_type=jnp.float32
    )


def left_matrix():
    pick = np.zeros((KEPT, TERMS), np.float32)
    block_of = {0: 0, 1: 1, 2: 3}
    for block, part in enumerate(LEFT_PARTS):
        for comp in range(3):
            pick[block_of[part] * BLOCK + comp, block * BLOCK + comp] = 0.5
    for part, block in ((0, 0), (1, 1), (2, 3)):
        pick[ONE_AT, block * BLOCK + NORM_AT] = 1.0
    for part, block in ((0, 0), (1, 2), (2, 4)):
        pick[block_of[part] * BLOCK + NORM_AT, block * BLOCK + ONE_AT] = 1.0
    return pick


def block_step(extent, slots):
    inner_x, inner_y, inner_z = extent
    ext_y, ext_z = inner_y + 2, inner_z + 2
    cells = (inner_x + 2) * ext_y * ext_z
    vert_x, vert_y, vert_z = inner_x + 1, inner_y + 1, inner_z + 1
    verts = vert_x * vert_y * vert_z
    rows8 = verts * 8
    spare = cells * slots // SPARE_ROWS
    lanes = 8 * slots
    group_size = next(size for size in (3, 2, 1) if verts % size == 0)

    def cell_of(cx, cy, cz):
        return (cx * ext_y + cy) * ext_z + cz

    def vert_of(vx, vy, vz):
        return (vx * vert_y + vy) * vert_z + vz

    def corner_cells(v):
        vz = v % vert_z
        vy = (v // vert_z) % vert_y
        vx = v // (vert_z * vert_y)
        return [cell_of(vx + (k >> 2), vy + ((k >> 1) & 1), vz + (k & 1)) for k in range(8)]

    def kernel(ext_ref, pos_ref, vel_ref, live_ref, pick_ref, vel_out, moved_out,
               corner, cell_rows, dest, count_rows, right, left, left_now, listed_now, left_t, grad_row, dens_lane, grad_lane, totals,
               spare_left, spare_left_t, spare_grad, spare_vert, spare_count, count_scalars, count_sem):
        sub = lax.broadcasted_iota(jnp.int32, (8, slots), 0)
        fill = jnp.where(sub == ONE_AT, 1.0, 0.0)
        for c in range(cells):
            cell_rows[c * 8 : c * 8 + 8, :] = fill
            cell_rows[c * 8 : c * 8 + 3, :] = ext_ref[c]
        for v in range(verts):
            for kxy, c in enumerate(corner_cells(v)[::2]):
                for comp in range(3):
                    corner[comp, v * 8 + 2 * kxy : v * 8 + 2 * kxy + 2, :] = ext_ref[c : c + 2, comp, :]

        row_id = lax.broadcasted_iota(jnp.int32, (rows8, slots), 0)
        near = None
        for comp in range(3):
            upper = ((row_id >> (2 - comp)) & 1) == 1
            x = corner[comp]
            low = x < HALF_EDGE
            test = jnp.where(upper, jnp.where(low, 1.0, 0.0), jnp.where(low | (x > 0.5 * FAR), 0.0, 1.0))
            near = test if near is None else near * test
        near_b = near.astype(jnp.bfloat16)
        lane_a = lax.broadcasted_iota(jnp.int32, (slots, slots), 0)
        lane_b = lax.broadcasted_iota(jnp.int32, (slots, slots), 1)
        before = jnp.where(lane_a < lane_b, 1.0, 0.0).astype(jnp.bfloat16)
        prefix = jnp.dot(near_b, before, preferred_element_type=jnp.float32)
        total = jnp.dot(near_b, jnp.ones((slots, slots), jnp.bfloat16), preferred_element_type=jnp.float32)
        wide_a = lax.broadcasted_iota(jnp.int32, (rows8, rows8), 0)
        wide_b = lax.broadcasted_iota(jnp.int32, (rows8, rows8), 1)
        earlier = jnp.where((wide_a >> 3 == wide_b >> 3) & (wide_b < wide_a), 1.0, 0.0).astype(jnp.bfloat16)
        offset = jnp.dot(earlier, total.astype(jnp.bfloat16), preferred_element_type=jnp.float32)
        dest[...] = jnp.where(near > 0.5, prefix + offset, -1.0)
        most = jnp.max(offset + total)
        count_rows[...] = (offset + total).astype(jnp.int32)
        dens_lane[...] = jnp.zeros(dens_lane.shape, jnp.float32)

        scale = jnp.where(sub < 3, 2.0 * SPREAD, jnp.where(sub == ONE_AT, 1.0, 0.0))
        shifts = []
        for k in range(8):
            low_side = jnp.zeros((8, slots), jnp.float32)
            for comp in range(3):
                if not (k >> (2 - comp)) & 1:
                    low_side = jnp.where(sub == comp, 2.0 * SPREAD * CELL_EDGE, low_side)
            shifts.append(low_side)

        def terms_of(v):
            packed = []
            for k, c in enumerate(corner_cells(v)):
                x = cell_rows[pl.ds(pl.multiple_of(c * 8, 8), 8), :] * scale - shifts[k]
                square = jnp.sum(x * x, axis=0, keepdims=True)
                x = jnp.where(sub == NORM_AT, 0.5 * TOP + 0.25 - 0.25 * square, x)
                parts = split_three(x)
                packed.append([
                    jnp.concatenate([parts[RIGHT_PARTS[b]], parts[RIGHT_PARTS[b + 1]]], axis=0).astype(jnp.bfloat16)
                    for b in (0, 2, 4)
                ])
            return packed

        def store_terms(v, packed):
            for k in range(8):
                for pair in range(3):
                    right[v, 16 * pair : 16 * pair + 16, k * slots : (k + 1) * slots] = packed[k][pair]

        def list_of(v, first_row, rows):
            place = (dest[pl.ds(pl.multiple_of(v * 8, 8), 8), :] - first_row).astype(jnp.bfloat16)
            row = lax.broadcasted_iota(jnp.int32, (rows, slots), 0).astype(jnp.float32).astype(jnp.bfloat16)
            one, none = jnp.ones((), jnp.bfloat16), jnp.zeros((), jnp.bfloat16)
            chosen = jnp.concatenate([jnp.where(row == place[k : k + 1, :], one, none) for k in range(8)], axis=1)
            near_right = right[v, 0:KEPT, :]
            listed = rows_of(1, 1, chosen, near_right)
            return listed.astype(jnp.bfloat16), listed.T.astype(jnp.bfloat16)

        def lefts_of(listed):
            return jnp.dot(listed, pick_ref[...], preferred_element_type=jnp.float32).astype(jnp.bfloat16)

        def grad_of(density_sum):
            density = density_sum * DENSITY_SCALE
            return (2.0 * GRAD_SCALE) * (density - (SCALE_DENSITY + DENSITY_REF))

        def density_of(v, lefts, rows):
            near_cells = corner_cells(v)
            sums = None
            for pair in range(4):
                both = jnp.dot(
                    lefts, right[v, :, 2 * pair * slots : (2 * pair + 2) * slots], preferred_element_type=jnp.float32
                )
                for side in range(2):
                    s = jnp.maximum(both[:, side * slots : (side + 1) * slots], 0.0)
                    part = jnp.exp2(s) * (s * s)
                    sums = part if sums is None else sums + part
                    dens_lane[near_cells[2 * pair + side]] += jnp.sum(part.reshape(rows // 8, 8, slots), axis=0)
            grad = grad_of(jnp.sum(sums, axis=1, keepdims=True))
            return jnp.broadcast_to(grad, (rows, slots))

        last = verts // group_size - 1

        def group_of(g):
            return [jnp.minimum(g, last) * group_size + i for i in range(group_size)]

        def store_group(terms=None, lists=None, lefts=None):
            if lefts is not None:
                for i, v in enumerate(lefts[0]):
                    left[v] = lefts[1][i]
                    left_now[i] = lefts[1][i]
            if lists is not None:
                for i, v in enumerate(lists[0]):
                    listed_now[i] = lists[1][i][0]
                    left_t[v] = lists[1][i][1]
            if terms is not None:
                for i, v in enumerate(terms[0]):
                    store_terms(v, terms[1][i])

        def make(g, maker):
            return group_of(g), [maker(v) for v in group_of(g)]

        def make_lists(v):
            return list_of(v, 0.0, ROWS)

        def make_lefts(g):
            return group_of(g), [lefts_of(listed_now[i]) for i in range(group_size)]

        def visit(g, carry):
            now = [left_now[i] for i in range(group_size)]
            lefts = make_lefts(g + 1)
            grads = []
            lists = (group_of(g + 2), [])
            terms = (group_of(g + 3), [])
            for i in range(group_size):
                grads.append(density_of(g * group_size + i, now[i], ROWS))
                lists[1].append(make_lists(lists[0][i]))
                terms[1].append(terms_of(terms[0][i]))
            for i in range(group_size):
                grad_row[g * group_size + i] = grads[i]
            store_group(terms, lists, lefts)
            return carry

        for g in range(3):
            store_group(terms=make(g, terms_of))
        store_group(lists=make(0, make_lists))
        store_group(lefts=make_lefts(0))
        store_group(lists=make(1, make_lists))
        lax.fori_loop(0, verts // group_size, visit, 0)
        spare_count[0] = 0

        @pl.when(most > ROWS)
        def _():
            copy = pltpu.make_async_copy(count_rows, count_scalars, count_sem)
            copy.start()
            copy.wait()

            def visit_vert(v, carry):
                count = count_scalars[v * 8 + 7, 0]

                def chunk(t, inner):
                    slot = spare_count[0]
                    spare_count[0] = slot + 1
                    spare_vert[slot] = v
                    first = ROWS + t * SPARE_ROWS
                    listed, listed_t = list_of(v, first.astype(jnp.float32), SPARE_ROWS)
                    lefts = lefts_of(listed)
                    spare_left[slot] = lefts
                    spare_left_t[slot] = listed_t
                    spare_grad[slot] = density_of(v, lefts, SPARE_ROWS)
                    return inner

                more = jnp.maximum(count - ROWS + SPARE_ROWS - 1, 0) // SPARE_ROWS
                return lax.fori_loop(0, more, chunk, carry)

            lax.fori_loop(0, verts, visit_vert, 0)

        for c in range(cells):
            grad_lane[c] = jnp.broadcast_to(grad_of(jnp.sum(dens_lane[c], axis=0, keepdims=True)), (8, slots))

        def force_sums(v, k, c, lefts, listed_t, grads):
            s = jnp.dot(lefts, right[v, :, k * slots : (k + 1) * slots], preferred_element_type=jnp.float32)
            s = jnp.maximum(s, 0.0)
            fall = jnp.exp2(s)
            both = grads + grad_lane[c, 0:1, :]
            push = (fall * s) * (fall * (s + PAIR_SHIFT) + both * (s + DENSITY_SHIFT))
            high = push.astype(jnp.bfloat16)
            low = (push - high.astype(jnp.float32)).astype(jnp.bfloat16)
            return rows_of(1, 0, listed_t, high) + rows_of(1, 0, listed_t, low)

        def shares(sums, k):
            weight = sums[ONE_AT : ONE_AT + 1, :]
            out = []
            for comp in range(3):
                moment = sums[comp : comp + 1, :] + sums[BLOCK + comp : BLOCK + comp + 1, :]
                moment = (moment + sums[3 * BLOCK + comp : 3 * BLOCK + comp + 1, :]) * (0.5 / SPREAD)
                if not (k >> (2 - comp)) & 1:
                    moment = moment + CELL_EDGE * weight
                out.append(moment)
            return out + [weight]

        def visit_cell(n, carry):
            iz = n % inner_z
            iy = (n // inner_z) % inner_y
            ix = n // (inner_z * inner_y)
            c = cell_of(ix + 1, iy + 1, iz + 1)
            gathered = None
            for k in range(8):
                v = vert_of(ix + 1 - (k >> 2), iy + 1 - ((k >> 1) & 1), iz + 1 - (k & 1))
                part = shares(force_sums(v, k, c, left[v], left_t[v], grad_row[v]), k)
                gathered = part if gathered is None else [a + b for a, b in zip(gathered, part)]
            totals[c] = jnp.concatenate(gathered + [jnp.zeros((4, slots), jnp.float32)], axis=0)
            return carry

        lax.fori_loop(0, inner_x * inner_y * inner_z, visit_cell, 0, unroll=2)

        def spare_force(e, carry):
            v = spare_vert[e]
            for k, c in enumerate(corner_cells(v)):
                part = shares(force_sums(v, k, c, spare_left[e], spare_left_t[e], spare_grad[e]), k)
                totals[c] += jnp.concatenate(part + [jnp.zeros((4, slots), jnp.float32)], axis=0)
            return carry

        lax.fori_loop(0, spare_count[0], spare_force, 0)

        for ix in range(inner_x):
            for iy in range(inner_y):
                c = cell_of(ix + 1, iy + 1, 1)
                n = (ix * inner_y + iy) * inner_z
                for iz in range(inner_z):
                    alive = live_ref[n + iz : n + iz + 1, :]
                    both = totals[c + iz]
                    for comp in range(3):
                        x = pos_ref[comp, n + iz : n + iz + 1, :]
                        force = FORCE_SCALE * (both[comp : comp + 1, :] - x * both[3:4, :])
                        velocity = vel_ref[comp, n + iz : n + iz + 1, :] + TIME_STEP * force
                        velocity = jnp.where(alive > 0.5, velocity, 0.0)
                        vel_out[comp, n + iz : n + iz + 1, :] = velocity
                        moved_out[comp, n + iz : n + iz + 1, :] = TIME_STEP * velocity

    own_cells = inner_x * inner_y * inner_z
    vmem = pl.BlockSpec(memory_space=pltpu.VMEM)
    pairs = verts * 8 * ROWS * slots
    return pl.pallas_call(
        kernel,
        out_shape=(jax.ShapeDtypeStruct((3, own_cells, slots), jnp.float32),) * 2,
        in_specs=[vmem] * 5,
        out_specs=(vmem, vmem),
        scratch_shapes=[
            pltpu.VMEM((3, rows8, slots), jnp.float32),
            pltpu.VMEM((cells * 8, slots), jnp.float32),
            pltpu.VMEM((rows8, slots), jnp.float32),
            pltpu.VMEM((rows8, slots), jnp.int32),
            pltpu.VMEM((verts, TERMS, lanes), jnp.bfloat16),
            pltpu.VMEM((verts, ROWS, TERMS), jnp.bfloat16),
            pltpu.VMEM((group_size, ROWS, TERMS), jnp.bfloat16),
            pltpu.VMEM((group_size, ROWS, KEPT), jnp.bfloat16),
            pltpu.VMEM((verts, KEPT, ROWS), jnp.bfloat16),
            pltpu.VMEM((verts, ROWS, slots), jnp.float32),
            pltpu.VMEM((cells, 8, slots), jnp.float32),
            pltpu.VMEM((cells, 8, slots), jnp.float32),
            pltpu.VMEM((cells, 8, slots), jnp.float32),
            pltpu.VMEM((spare, SPARE_ROWS, TERMS), jnp.bfloat16),
            pltpu.VMEM((spare, KEPT, SPARE_ROWS), jnp.bfloat16),
            pltpu.VMEM((spare, SPARE_ROWS, slots), jnp.float32),
            pltpu.SMEM((spare,), jnp.int32),
            pltpu.SMEM((1,), jnp.int32),
            pltpu.SMEM((rows8, slots), jnp.int32),
            pltpu.SemaphoreType.DMA,
        ],
        compiler_params=pltpu.CompilerParams(vmem_limit_bytes=60 * 2**20),
        cost_estimate=pl.CostEstimate(flops=40 * pairs, bytes_accessed=4 * 3 * cells * slots, transcendentals=2 * pairs),
        name="block_step",
    )


def body(positions, velocities, counts):
    comps, size_x, size_y, size_z, slots = positions.shape
    own_cells = size_x * size_y * size_z
    slot_index = lax.broadcasted_iota(jnp.int32, counts.shape + (slots,), 3)
    live = slot_index < counts[..., None]
    shown = jnp.where(live[..., None, :], positions.transpose(1, 2, 3, 0, 4), FAR)
    ext = with_halo(shown)
    step = block_step((size_x, size_y, size_z), slots)
    velocity, moved = step(
        ext.reshape(-1, comps, slots),
        positions.reshape(comps, own_cells, slots),
        velocities.reshape(comps, own_cells, slots),
        live.astype(jnp.float32).reshape(own_cells, slots),
        jnp.asarray(left_matrix(), jnp.bfloat16),
    )
    return velocity.reshape(positions.shape), moved.reshape(positions.shape)


def solution(mesh):
    spec = P(None, *AXES, None)
    return jax.shard_map(
        body,
        mesh=mesh,
        in_specs=(spec, spec, P(*AXES)),
        out_specs=(spec, spec),
        check_vma=False,
    )
```

```python
import math
import jax
import jax.numpy as jnp
import numpy as np
from jax import lax
from jax.experimental import pallas as pl
from jax.experimental.pallas import tpu as pltpu
from jax.sharding import PartitionSpec as P

CELL_EDGE = 11.0
HALF_EDGE = 5.5
CUT_SQ = 25.0
WIDTH_DENSITY = 4.0
WIDTH_PAIR = 2.0
SCALE_DENSITY = 0.4
SCALE_PAIR = 0.3
DENSITY_REF = 1.0
TIME_STEP = 0.5
FAR = 4096.0
AXES = ("gx", "gy", "gz")

TOP_E = CUT_SQ / WIDTH_DENSITY
TOP = TOP_E / math.log(2.0)
SPREAD = math.sqrt(TOP / CUT_SQ)
DENSITY_SCALE = SCALE_DENSITY * math.exp(-TOP_E) / TOP**2
PAIR_SHIFT = 4.0 * TOP / CUT_SQ
DENSITY_SHIFT = 8.0 * TOP / CUT_SQ
FORCE_SCALE = -SCALE_PAIR * math.exp(-2.0 * TOP_E) / TOP**2
GRAD_SCALE = SCALE_DENSITY / (2.0 * SCALE_PAIR) * math.exp(TOP_E)

ROWS = 144
SPARE_ROWS = 32
FORCE_UNROLL = 4
LEFT_PARTS = (0, 0, 1, 0, 2, 1)
RIGHT_PARTS = (0, 1, 0, 2, 0, 1)
BLOCK = 8
TERMS = 6 * BLOCK
KEPT = 4 * BLOCK
NORM_AT = 3
ONE_AT = 4


def neighbour_layers(field, axis, name):
    count = lax.axis_size(name)
    size = field.shape[axis]
    first = lax.slice_in_dim(field, 0, 1, axis=axis)
    last = lax.slice_in_dim(field, size - 1, size, axis=axis)
    if count == 1:
        return last, first
    if count == 2:
        swapped = lax.ppermute(jnp.concatenate([last, first], axis=axis), name, [(0, 1), (1, 0)])
        return lax.slice_in_dim(swapped, 0, 1, axis=axis), lax.slice_in_dim(swapped, 1, 2, axis=axis)
    below = lax.ppermute(last, name, [(d, (d + 1) % count) for d in range(count)])
    above = lax.ppermute(first, name, [(d, (d - 1) % count) for d in range(count)])
    return below, above


def with_halo(field):
    for axis, name in enumerate(AXES, 1):
        below, above = neighbour_layers(field, axis, name)
        field = jnp.concatenate([below, field, above], axis=axis)
    return field


def split_three(value):
    high = value.astype(jnp.bfloat16).astype(jnp.float32)
    rest = value - high
    middle = rest.astype(jnp.bfloat16).astype(jnp.float32)
    return high, middle, rest - middle


def rows_of(contract_a, contract_b, a, b):
    return lax.dot_general(
        a, b, (((contract_a,), (contract_b,)), ((), ())), preferred_element_type=jnp.float32
    )


def left_matrix():
    pick = np.zeros((KEPT, TERMS), np.float32)
    block_of = {0: 0, 1: 1, 2: 3}
    for block, part in enumerate(LEFT_PARTS):
        for comp in range(3):
            pick[block_of[part] * BLOCK + comp, block * BLOCK + comp] = 0.5
    for part, block in ((0, 0), (1, 1), (2, 3)):
        pick[ONE_AT, block * BLOCK + NORM_AT] = 1.0
    for part, block in ((0, 0), (1, 2), (2, 4)):
        pick[block_of[part] * BLOCK + NORM_AT, block * BLOCK + ONE_AT] = 1.0
    return pick


def block_step(extent, slots):
    inner_x, inner_y, inner_z = extent
    ext_y, ext_z = inner_y + 2, inner_z + 2
    cells = (inner_x + 2) * ext_y * ext_z
    vert_x, vert_y, vert_z = inner_x + 1, inner_y + 1, inner_z + 1
    verts = vert_x * vert_y * vert_z
    rows8 = verts * 8
    spare = cells * slots // SPARE_ROWS
    lanes = 8 * slots
    group_size = next(size for size in (5, 3, 2, 1) if verts % size == 0)

    def cell_of(cx, cy, cz):
        return (cx * ext_y + cy) * ext_z + cz

    def vert_of(vx, vy, vz):
        return (vx * vert_y + vy) * vert_z + vz

    def corner_cells(v):
        vz = v % vert_z
        vy = (v // vert_z) % vert_y
        vx = v // (vert_z * vert_y)
        return [cell_of(vx + (k >> 2), vy + ((k >> 1) & 1), vz + (k & 1)) for k in range(8)]

    def kernel(ext_ref, pos_ref, vel_ref, count_ref, pick_ref, vel_out, moved_out,
               corner, cell_rows, dest, count_rows, right, left, left_now, listed_now, left_t, grad_row, dens_lane, grad_lane, totals,
               spare_left, spare_left_t, spare_grad, spare_vert, spare_count, count_scalars, count_sem):
        sub = lax.broadcasted_iota(jnp.int32, (8, slots), 0)
        fill = jnp.where(sub == ONE_AT, 1.0, 0.0)
        for cx in range(inner_x + 2):
            for cy in range(ext_y):
                for cz in range(ext_z):
                    c = cell_of(cx, cy, cz)
                    cell_rows[c * 8 : c * 8 + 8, :] = fill
                    for comp in range(3):
                        cell_rows[c * 8 + comp : c * 8 + comp + 1, :] = ext_ref[comp, cx, cy, cz : cz + 1, :]
        for v in range(verts):
            vx, vy, vz = v // (vert_z * vert_y), (v // vert_z) % vert_y, v % vert_z
            for kxy in range(4):
                for comp in range(3):
                    corner[comp, v * 8 + 2 * kxy : v * 8 + 2 * kxy + 2, :] = ext_ref[
                        comp, vx + kxy // 2, vy + kxy % 2, vz : vz + 2, :
                    ]

        row_id = lax.broadcasted_iota(jnp.int32, (rows8, slots), 0)
        near = None
        for comp in range(3):
            upper = ((row_id >> (2 - comp)) & 1) == 1
            x = corner[comp]
            low = x < HALF_EDGE
            test = jnp.where(upper, jnp.where(low, 1.0, 0.0), jnp.where(low | (x > 0.5 * FAR), 0.0, 1.0))
            near = test if near is None else near * test
        near_b = near.astype(jnp.bfloat16)
        lane_a = lax.broadcasted_iota(jnp.int32, (slots, slots), 0)
        lane_b = lax.broadcasted_iota(jnp.int32, (slots, slots), 1)
        before = jnp.where(lane_a < lane_b, 1.0, 0.0).astype(jnp.bfloat16)
        prefix = jnp.dot(near_b, before, preferred_element_type=jnp.float32)
        total = jnp.dot(near_b, jnp.ones((slots, slots), jnp.bfloat16), preferred_element_type=jnp.float32)
        wide_a = lax.broadcasted_iota(jnp.int32, (rows8, rows8), 0)
        wide_b = lax.broadcasted_iota(jnp.int32, (rows8, rows8), 1)
        earlier = jnp.where((wide_a >> 3 == wide_b >> 3) & (wide_b < wide_a), 1.0, 0.0).astype(jnp.bfloat16)
        offset = jnp.dot(earlier, total.astype(jnp.bfloat16), preferred_element_type=jnp.float32)
        dest[...] = jnp.where(near > 0.5, prefix + offset, -1.0)
        most = jnp.max(offset + total)
        listed_to = offset + total
        dens_lane[...] = jnp.zeros(dens_lane.shape, jnp.float32)

        scale = jnp.where(sub < 3, 2.0 * SPREAD, jnp.where(sub == ONE_AT, 1.0, 0.0))
        shifts = []
        for k in range(8):
            low_side = jnp.zeros((8, slots), jnp.float32)
            for comp in range(3):
                if not (k >> (2 - comp)) & 1:
                    low_side = jnp.where(sub == comp, 2.0 * SPREAD * CELL_EDGE, low_side)
            shifts.append(low_side)

        def terms_of(v):
            packed = []
            for k, c in enumerate(corner_cells(v)):
                x = cell_rows[pl.ds(pl.multiple_of(c * 8, 8), 8), :] * scale - shifts[k]
                square = jnp.sum(x * x, axis=0, keepdims=True)
                x = jnp.where(sub == NORM_AT, 0.5 * TOP + 0.25 - 0.25 * square, x)
                parts = split_three(x)
                packed.append([
                    jnp.concatenate([parts[RIGHT_PARTS[b]], parts[RIGHT_PARTS[b + 1]]], axis=0).astype(jnp.bfloat16)
                    for b in (0, 2, 4)
                ])
            return packed

        def store_terms(v, packed):
            for k in range(8):
                for pair in range(3):
                    right[v, 16 * pair : 16 * pair + 16, k * slots : (k + 1) * slots] = packed[k][pair]

        def list_of(v, first_row, rows):
            place = (dest[pl.ds(pl.multiple_of(v * 8, 8), 8), :] - first_row).astype(jnp.bfloat16)
            row = lax.broadcasted_iota(jnp.int32, (rows, slots), 0).astype(jnp.float32).astype(jnp.bfloat16)
            one, none = jnp.ones((), jnp.bfloat16), jnp.zeros((), jnp.bfloat16)
            chosen = jnp.concatenate([jnp.where(row == place[k : k + 1, :], one, none) for k in range(8)], axis=1)
            near_right = right[v, 0:KEPT, :]
            listed = rows_of(1, 1, chosen, near_right)
            return listed.astype(jnp.bfloat16), listed.T.astype(jnp.bfloat16)

        def lefts_of(listed):
            return jnp.dot(listed, pick_ref[...], preferred_element_type=jnp.float32).astype(jnp.bfloat16)

        def grad_of(density_sum):
            density = density_sum * DENSITY_SCALE
            return (2.0 * GRAD_SCALE) * (density - (SCALE_DENSITY + DENSITY_REF))

        def density_of(v, lefts, rows):
            near_cells = corner_cells(v)
            sums = None
            for pair in range(4):
                both = jnp.dot(
                    lefts, right[v, :, 2 * pair * slots : (2 * pair + 2) * slots], preferred_element_type=jnp.float32
                )
                for side in range(2):
                    s = jnp.maximum(both[:, side * slots : (side + 1) * slots], 0.0)
                    part = jnp.exp2(s) * (s * s)
                    sums = part if sums is None else sums + part
                    dens_lane[near_cells[2 * pair + side]] += jnp.sum(part.reshape(rows // 8, 8, slots), axis=0)
            grad = grad_of(jnp.sum(sums, axis=1, keepdims=True))
            return jnp.broadcast_to(grad, (rows, slots))

        last = verts // group_size - 1

        def group_of(g):
            return [jnp.minimum(g, last) * group_size + i for i in range(group_size)]

        def store_group(lists=None, lefts=None):
            if lefts is not None:
                for i, v in enumerate(lefts[0]):
                    left[v] = lefts[1][i]
                    left_now[i] = lefts[1][i]
            if lists is not None:
                for i, v in enumerate(lists[0]):
                    listed_now[i] = lists[1][i][0]
                    left_t[v] = lists[1][i][1]

        def make(g, maker):
            return group_of(g), [maker(v) for v in group_of(g)]

        def make_lists(v):
            return list_of(v, 0.0, ROWS)

        def make_lefts(g):
            return group_of(g), [lefts_of(listed_now[i]) for i in range(group_size)]

        def visit(g, carry):
            now = [left_now[i] for i in range(group_size)]
            lefts = make_lefts(g + 1)
            grads = []
            lists = (group_of(g + 2), [])
            for i in range(group_size):
                grads.append(density_of(g * group_size + i, now[i], ROWS))
                lists[1].append(make_lists(lists[0][i]))
            for i in range(group_size):
                grad_row[g * group_size + i] = grads[i]
            store_group(lists, lefts)
            return carry

        def visit_terms(g, carry):
            packed = make(g, terms_of)
            for i, v in enumerate(packed[0]):
                store_terms(v, packed[1][i])
            return carry

        lax.fori_loop(0, verts // group_size, visit_terms, 0)
        store_group(lists=make(0, make_lists))
        store_group(lefts=make_lefts(0))
        store_group(lists=make(1, make_lists))
        lax.fori_loop(0, verts // group_size, visit, 0)
        spare_count[0] = 0

        @pl.when(most > ROWS)
        def _():
            lane_id = lax.broadcasted_iota(jnp.int32, (rows8, slots), 1)
            ends = jnp.where((row_id & 7 == 7) & (row_id >> 3 == lane_id), listed_to, 0.0)
            ends = jnp.sum(ends, axis=0, keepdims=True)
            count_rows[...] = jnp.broadcast_to(ends, (8, slots)).astype(jnp.int32)
            copy = pltpu.make_async_copy(count_rows, count_scalars, count_sem)
            copy.start()
            copy.wait()

            def visit_vert(v, carry):
                count = count_scalars[0, v]

                def chunk(t, inner):
                    slot = spare_count[0]
                    spare_count[0] = slot + 1
                    spare_vert[slot] = v
                    first = ROWS + t * SPARE_ROWS
                    listed, listed_t = list_of(v, first.astype(jnp.float32), SPARE_ROWS)
                    lefts = lefts_of(listed)
                    spare_left[slot] = lefts
                    spare_left_t[slot] = listed_t
                    spare_grad[slot] = density_of(v, lefts, SPARE_ROWS)
                    return inner

                more = jnp.maximum(count - ROWS + SPARE_ROWS - 1, 0) // SPARE_ROWS
                return lax.fori_loop(0, more, chunk, carry)

            lax.fori_loop(0, verts, visit_vert, 0)

        for c in range(cells):
            grad_lane[c] = jnp.broadcast_to(grad_of(jnp.sum(dens_lane[c], axis=0, keepdims=True)), (8, slots))

        def force_sums(v, k, c, lefts, listed_t, grads):
            s = jnp.dot(lefts, right[v, :, k * slots : (k + 1) * slots], preferred_element_type=jnp.float32)
            s = jnp.maximum(s, 0.0)
            fall = jnp.exp2(s)
            both = grads + grad_lane[c, 0:1, :]
            push = (fall * s) * (fall * (s + PAIR_SHIFT) + both * (s + DENSITY_SHIFT))
            high = push.astype(jnp.bfloat16)
            low = (push - high.astype(jnp.float32)).astype(jnp.bfloat16)
            return rows_of(1, 0, listed_t, high) + rows_of(1, 0, listed_t, low)

        def shares(sums):
            weight = sum(s[ONE_AT : ONE_AT + 1, :] for s in sums)
            whole = sum(sums)
            out = []
            for comp in range(3):
                moment = whole[comp : comp + 1, :] + whole[BLOCK + comp : BLOCK + comp + 1, :]
                moment = (moment + whole[3 * BLOCK + comp : 3 * BLOCK + comp + 1, :]) * (0.5 / SPREAD)
                low_side = sum(sums[k][ONE_AT : ONE_AT + 1, :] for k in range(8) if not (k >> (2 - comp)) & 1)
                out.append(moment + CELL_EDGE * low_side)
            return jnp.concatenate(out + [weight, jnp.zeros((4, slots), jnp.float32)], axis=0)

        def visit_cell(n, carry):
            iz = n % inner_z
            iy = (n // inner_z) % inner_y
            ix = n // (inner_z * inner_y)
            c = cell_of(ix + 1, iy + 1, iz + 1)
            sums = []
            for k in range(8):
                v = vert_of(ix + 1 - (k >> 2), iy + 1 - ((k >> 1) & 1), iz + 1 - (k & 1))
                sums.append(force_sums(v, k, c, left[v], left_t[v], grad_row[v]))
            totals[c] = shares(sums)
            return carry

        lax.fori_loop(0, inner_x * inner_y * inner_z, visit_cell, 0, unroll=FORCE_UNROLL)

        def spare_force(e, carry):
            v = spare_vert[e]
            none = jnp.zeros((KEPT, slots), jnp.float32)
            for k, c in enumerate(corner_cells(v)):
                sums = force_sums(v, k, c, spare_left[e], spare_left_t[e], spare_grad[e])
                totals[c] += shares([sums if k == place else none for place in range(8)])
            return carry

        lax.fori_loop(0, spare_count[0], spare_force, 0)

        slot_id = lax.broadcasted_iota(jnp.int32, (1, slots), 1)
        for ix in range(inner_x):
            for iy in range(inner_y):
                c = cell_of(ix + 1, iy + 1, 1)
                n = (ix * inner_y + iy) * inner_z
                for iz in range(inner_z):
                    alive = slot_id < count_ref[n + iz]
                    both = totals[c + iz]
                    for comp in range(3):
                        x = pos_ref[comp, n + iz : n + iz + 1, :]
                        force = FORCE_SCALE * (both[comp : comp + 1, :] - x * both[3:4, :])
                        velocity = vel_ref[comp, n + iz : n + iz + 1, :] + TIME_STEP * force
                        velocity = jnp.where(alive, velocity, 0.0)
                        vel_out[comp, n + iz : n + iz + 1, :] = velocity
                        moved_out[comp, n + iz : n + iz + 1, :] = TIME_STEP * velocity

    own_cells = inner_x * inner_y * inner_z
    vmem = pl.BlockSpec(memory_space=pltpu.VMEM)
    pairs = verts * 8 * ROWS * slots
    return pl.pallas_call(
        kernel,
        out_shape=(jax.ShapeDtypeStruct((3, own_cells, slots), jnp.float32),) * 2,
        in_specs=[vmem] * 3 + [pl.BlockSpec(memory_space=pltpu.SMEM), vmem],
        out_specs=(vmem, vmem),
        scratch_shapes=[
            pltpu.VMEM((3, rows8, slots), jnp.float32),
            pltpu.VMEM((cells * 8, slots), jnp.float32),
            pltpu.VMEM((rows8, slots), jnp.float32),
            pltpu.VMEM((8, slots), jnp.int32),
            pltpu.VMEM((verts, TERMS, lanes), jnp.bfloat16),
            pltpu.VMEM((verts, ROWS, TERMS), jnp.bfloat16),
            pltpu.VMEM((group_size, ROWS, TERMS), jnp.bfloat16),
            pltpu.VMEM((group_size, ROWS, KEPT), jnp.bfloat16),
            pltpu.VMEM((verts, KEPT, ROWS), jnp.bfloat16),
            pltpu.VMEM((verts, ROWS, slots), jnp.float32),
            pltpu.VMEM((cells, 8, slots), jnp.float32),
            pltpu.VMEM((cells, 8, slots), jnp.float32),
            pltpu.VMEM((cells, 8, slots), jnp.float32),
            pltpu.VMEM((spare, SPARE_ROWS, TERMS), jnp.bfloat16),
            pltpu.VMEM((spare, KEPT, SPARE_ROWS), jnp.bfloat16),
            pltpu.VMEM((spare, SPARE_ROWS, slots), jnp.float32),
            pltpu.SMEM((spare,), jnp.int32),
            pltpu.SMEM((1,), jnp.int32),
            pltpu.SMEM((8, slots), jnp.int32),
            pltpu.SemaphoreType.DMA,
        ],
        compiler_params=pltpu.CompilerParams(vmem_limit_bytes=60 * 2**20),
        cost_estimate=pl.CostEstimate(flops=40 * pairs, bytes_accessed=4 * 3 * cells * slots, transcendentals=2 * pairs),
        name="block_step",
    )


def body(positions, velocities, counts):
    comps, size_x, size_y, size_z, slots = positions.shape
    own_cells = size_x * size_y * size_z
    slot_index = lax.broadcasted_iota(jnp.int32, counts.shape + (slots,), 3)
    live = slot_index < counts[..., None]
    shown = jnp.where(live[None], positions, FAR)
    ext = with_halo(shown)
    step = block_step((size_x, size_y, size_z), slots)
    velocity, moved = step(
        ext,
        positions.reshape(comps, own_cells, slots),
        velocities.reshape(comps, own_cells, slots),
        counts.reshape(own_cells),
        jnp.asarray(left_matrix(), jnp.bfloat16),
    )
    return velocity.reshape(positions.shape), moved.reshape(positions.shape)


def solution(mesh):
    spec = P(None, *AXES, None)
    return jax.shard_map(
        body,
        mesh=mesh,
        in_specs=(spec, spec, P(*AXES)),
        out_specs=(spec, spec),
        check_vma=False,
    )
```

```python
import math
import jax
import jax.numpy as jnp
import numpy as np
from jax import lax
from jax.experimental import pallas as pl
from jax.experimental.pallas import tpu as pltpu
from jax.sharding import PartitionSpec as P

CELL_EDGE = 11.0
HALF_EDGE = 5.5
CUT_SQ = 25.0
WIDTH_DENSITY = 4.0
WIDTH_PAIR = 2.0
SCALE_DENSITY = 0.4
SCALE_PAIR = 0.3
DENSITY_REF = 1.0
TIME_STEP = 0.5
FAR = 4096.0
AXES = ("gx", "gy", "gz")

TOP_E = CUT_SQ / WIDTH_DENSITY
TOP = TOP_E / math.log(2.0)
SPREAD = math.sqrt(TOP / CUT_SQ)
DENSITY_SCALE = SCALE_DENSITY * math.exp(-TOP_E) / TOP**2
PAIR_SHIFT = 4.0 * TOP / CUT_SQ
DENSITY_SHIFT = 8.0 * TOP / CUT_SQ
FORCE_SCALE = -SCALE_PAIR * math.exp(-2.0 * TOP_E) / TOP**2
GRAD_SCALE = SCALE_DENSITY / (2.0 * SCALE_PAIR) * math.exp(TOP_E)

ROWS = 144
SPARE_ROWS = 32
LEFT_PARTS = (0, 0, 1, 0, 2, 1)
RIGHT_PARTS = (0, 1, 0, 2, 0, 1)
BLOCK = 8
TERMS = 6 * BLOCK
KEPT = 4 * BLOCK
NORM_AT = 3
ONE_AT = 4


def neighbour_layers(field, axis, name):
    count = lax.axis_size(name)
    size = field.shape[axis]
    first = lax.slice_in_dim(field, 0, 1, axis=axis)
    last = lax.slice_in_dim(field, size - 1, size, axis=axis)
    if count == 1:
        return last, first
    if count == 2:
        swapped = lax.ppermute(jnp.concatenate([last, first], axis=axis), name, [(0, 1), (1, 0)])
        return lax.slice_in_dim(swapped, 0, 1, axis=axis), lax.slice_in_dim(swapped, 1, 2, axis=axis)
    below = lax.ppermute(last, name, [(d, (d + 1) % count) for d in range(count)])
    above = lax.ppermute(first, name, [(d, (d - 1) % count) for d in range(count)])
    return below, above


def with_halo(field):
    for axis, name in enumerate(AXES, 1):
        below, above = neighbour_layers(field, axis, name)
        field = jnp.concatenate([below, field, above], axis=axis)
    return field


def split_three(value):
    high = value.astype(jnp.bfloat16).astype(jnp.float32)
    rest = value - high
    middle = rest.astype(jnp.bfloat16).astype(jnp.float32)
    return high, middle, rest - middle


def rows_of(contract_a, contract_b, a, b):
    return lax.dot_general(
        a, b, (((contract_a,), (contract_b,)), ((), ())), preferred_element_type=jnp.float32
    )


def left_matrix():
    pick = np.zeros((KEPT, TERMS), np.float32)
    block_of = {0: 0, 1: 1, 2: 3}
    for block, part in enumerate(LEFT_PARTS):
        for comp in range(3):
            pick[block_of[part] * BLOCK + comp, block * BLOCK + comp] = 0.5
    for part, block in ((0, 0), (1, 1), (2, 3)):
        pick[ONE_AT, block * BLOCK + NORM_AT] = 1.0
    for part, block in ((0, 0), (1, 2), (2, 4)):
        pick[block_of[part] * BLOCK + NORM_AT, block * BLOCK + ONE_AT] = 1.0
    return pick.T


def block_step(extent, slots):
    inner_x, inner_y, inner_z = extent
    ext_y, ext_z = inner_y + 2, inner_z + 2
    cells = (inner_x + 2) * ext_y * ext_z
    vert_x, vert_y, vert_z = inner_x + 1, inner_y + 1, inner_z + 1
    verts = vert_x * vert_y * vert_z
    rows8 = verts * 8
    spare = cells * slots // SPARE_ROWS
    lanes = 8 * slots
    group_size = next(size for size in (5, 3, 2, 1) if verts % size == 0)

    def cell_of(cx, cy, cz):
        return (cx * ext_y + cy) * ext_z + cz

    def vert_of(vx, vy, vz):
        return (vx * vert_y + vy) * vert_z + vz

    def corner_cells(v):
        vz = v % vert_z
        vy = (v // vert_z) % vert_y
        vx = v // (vert_z * vert_y)
        return [cell_of(vx + (k >> 2), vy + ((k >> 1) & 1), vz + (k & 1)) for k in range(8)]

    def kernel(ext_ref, pos_ref, vel_ref, count_ref, pick_ref, vel_out, moved_out,
               corner, cell_rows, dest, count_rows, right, left, left_now, listed_now, left_t, grad_row, dens_lane, grad_lane, totals,
               spare_left, spare_left_t, spare_grad, spare_vert, spare_count):
        sub = lax.broadcasted_iota(jnp.int32, (8, slots), 0)
        fill = jnp.where(sub == ONE_AT, 1.0, 0.0)
        for cx in range(inner_x + 2):
            for cy in range(ext_y):
                for cz in range(ext_z):
                    c = cell_of(cx, cy, cz)
                    cell_rows[c * 8 : c * 8 + 8, :] = fill
                    for comp in range(3):
                        cell_rows[c * 8 + comp : c * 8 + comp + 1, :] = ext_ref[comp, cx, cy, cz : cz + 1, :]
        for v in range(verts):
            vx, vy, vz = v // (vert_z * vert_y), (v // vert_z) % vert_y, v % vert_z
            for kxy in range(4):
                for comp in range(3):
                    corner[comp, v * 8 + 2 * kxy : v * 8 + 2 * kxy + 2, :] = ext_ref[
                        comp, vx + kxy // 2, vy + kxy % 2, vz : vz + 2, :
                    ]

        row_id = lax.broadcasted_iota(jnp.int32, (rows8, slots), 0)
        near = None
        for comp in range(3):
            upper = ((row_id >> (2 - comp)) & 1) == 1
            x = corner[comp]
            low = x < HALF_EDGE
            test = jnp.where(upper, jnp.where(low, 1.0, 0.0), jnp.where(low | (x > 0.5 * FAR), 0.0, 1.0))
            near = test if near is None else near * test
        near_b = near.astype(jnp.bfloat16)
        lane_a = lax.broadcasted_iota(jnp.int32, (slots, slots), 0)
        lane_b = lax.broadcasted_iota(jnp.int32, (slots, slots), 1)
        before = jnp.where(lane_a < lane_b, 1.0, 0.0).astype(jnp.bfloat16)
        prefix = jnp.dot(near_b, before, preferred_element_type=jnp.float32)
        total = jnp.dot(near_b, jnp.ones((slots, slots), jnp.bfloat16), preferred_element_type=jnp.float32)
        earlier = jnp.where((lane_a >> 3 == lane_b >> 3) & (lane_b < lane_a), 1.0, 0.0).astype(jnp.bfloat16)
        offset = []
        for first in range(0, rows8, slots):
            size = min(slots, rows8 - first)
            offset.append(
                jnp.dot(
                    earlier[:size, :size], total[first : first + size, :].astype(jnp.bfloat16),
                    preferred_element_type=jnp.float32,
                )
            )
        offset = jnp.concatenate(offset, axis=0)
        dest[...] = jnp.where(near > 0.5, prefix + offset, -1.0)
        most = jnp.max(offset + total)
        listed_to = offset + total
        dens_lane[...] = jnp.zeros(dens_lane.shape, jnp.float32)

        scale = jnp.where(sub < 3, 2.0 * SPREAD, jnp.where(sub == ONE_AT, 1.0, 0.0))
        shifts = []
        for k in range(8):
            low_side = jnp.zeros((8, slots), jnp.float32)
            for comp in range(3):
                if not (k >> (2 - comp)) & 1:
                    low_side = jnp.where(sub == comp, 2.0 * SPREAD * CELL_EDGE, low_side)
            shifts.append(low_side)

        def terms_of(v):
            packed = []
            for k, c in enumerate(corner_cells(v)):
                x = cell_rows[pl.ds(pl.multiple_of(c * 8, 8), 8), :] * scale - shifts[k]
                square = jnp.sum(x * x, axis=0, keepdims=True)
                x = jnp.where(sub == NORM_AT, 0.5 * TOP + 0.25 - 0.25 * square, x)
                parts = split_three(x)
                packed.append([
                    jnp.concatenate([parts[RIGHT_PARTS[b]], parts[RIGHT_PARTS[b + 1]]], axis=0).astype(jnp.bfloat16)
                    for b in (0, 2, 4)
                ])
            return packed

        def store_terms(v, packed):
            for k in range(8):
                for pair in range(3):
                    right[v, 16 * pair : 16 * pair + 16, k * slots : (k + 1) * slots] = packed[k][pair]

        def list_of(v, first_row, rows):
            place = (dest[pl.ds(pl.multiple_of(v * 8, 8), 8), :] - first_row).astype(jnp.bfloat16)
            row = lax.broadcasted_iota(jnp.int32, (rows, slots), 0).astype(jnp.float32).astype(jnp.bfloat16)
            one, none = jnp.ones((), jnp.bfloat16), jnp.zeros((), jnp.bfloat16)
            chosen = jnp.concatenate([jnp.where(row == place[k : k + 1, :], one, none) for k in range(8)], axis=1)
            return rows_of(1, 1, right[v, 0:KEPT, :], chosen).astype(jnp.bfloat16)

        def lefts_of(listed_t):
            lefts_t = jnp.dot(pick_ref[...], listed_t, preferred_element_type=jnp.float32)
            return lefts_t.T.astype(jnp.bfloat16)

        def grad_of(density_sum):
            density = density_sum * DENSITY_SCALE
            return (2.0 * GRAD_SCALE) * (density - (SCALE_DENSITY + DENSITY_REF))

        def density_of(v, lefts, rows):
            near_cells = corner_cells(v)
            sums = None
            for pair in range(4):
                both = jnp.dot(
                    lefts, right[v, :, 2 * pair * slots : (2 * pair + 2) * slots], preferred_element_type=jnp.float32
                )
                for side in range(2):
                    s = jnp.maximum(both[:, side * slots : (side + 1) * slots], 0.0)
                    part = jnp.exp2(s) * (s * s)
                    sums = part if sums is None else sums + part
                    dens_lane[near_cells[2 * pair + side]] += jnp.sum(part.reshape(rows // 8, 8, slots), axis=0)
            grad = grad_of(jnp.sum(sums, axis=1, keepdims=True))
            return jnp.broadcast_to(grad, (rows, slots))

        groups = verts // group_size

        def group_of(g):
            return [g * group_size + i for i in range(group_size)]

        def visit_terms(g, carry):
            packed = [terms_of(v) for v in group_of(g)]
            for i, v in enumerate(group_of(g)):
                store_terms(v, packed[i])
            return carry

        def store_lists(g, lists):
            for i, v in enumerate(group_of(g)):
                listed_now[i] = lists[i]
                left_t[v] = lists[i]

        def store_lefts(g, lefts):
            for i, v in enumerate(group_of(g)):
                left_now[i] = lefts[i]
                left[v] = lefts[i]

        def store_grads(g, grads):
            for i, v in enumerate(group_of(g)):
                grad_row[v] = grads[i]

        def visit(g, carry):
            now = [left_now[i] for i in range(group_size)]
            lefts = [lefts_of(listed_now[i]) for i in range(group_size)]
            grads, lists = [], []
            for i in range(group_size):
                grads.append(density_of(group_of(g)[i], now[i], ROWS))
                lists.append(list_of(group_of(g + 2)[i], 0.0, ROWS))
            store_grads(g, grads)
            store_lefts(g + 1, lefts)
            store_lists(g + 2, lists)
            return carry

        def visit_last(g, carry):
            store_grads(g, [density_of(v, left[v], ROWS) for v in group_of(g)])
            return carry

        lax.fori_loop(0, groups, visit_terms, 0)
        first = [list_of(v, 0.0, ROWS) for v in group_of(0)]
        store_lists(0, first)
        store_lefts(0, [lefts_of(listed_t) for listed_t in first])
        if groups > 1:
            store_lists(1, [list_of(v, 0.0, ROWS) for v in group_of(1)])
        lax.fori_loop(0, max(groups - 2, 0), visit, 0)
        if groups > 1:
            for i, v in enumerate(group_of(groups - 1)):
                left[v] = lefts_of(listed_now[i])
        lax.fori_loop(max(groups - 2, 0), groups, visit_last, 0)
        spare_count[0] = 0

        @pl.when(most > ROWS)
        def _():
            lane_id = lax.broadcasted_iota(jnp.int32, (rows8, slots), 1)
            ends = jnp.where((row_id & 7 == 7) & (row_id >> 3 == lane_id), listed_to, 0.0)
            count_rows[...] = jnp.broadcast_to(jnp.sum(ends, axis=0, keepdims=True), (8, slots))
            grad_lane[...] = jnp.zeros(grad_lane.shape, jnp.float32)
            vert_id = lax.broadcasted_iota(jnp.int32, (8, slots), 1).astype(jnp.float32)

            def long_below(v):
                wanted = (count_rows[...] > ROWS) & (vert_id < v.astype(jnp.float32))
                return jnp.max(jnp.where(wanted, vert_id, -1.0)).astype(jnp.int32)

            def visit_vert(v):
                count = jnp.max(jnp.where(vert_id == v.astype(jnp.float32), count_rows[...], 0.0)).astype(jnp.int32)

                def chunk(t, inner):
                    slot = spare_count[0]
                    spare_count[0] = slot + 1
                    spare_vert[slot] = v
                    first = ROWS + t * SPARE_ROWS
                    listed_t = list_of(v, first.astype(jnp.float32), SPARE_ROWS)
                    lefts = lefts_of(listed_t)
                    spare_left[slot] = lefts
                    spare_left_t[slot] = listed_t
                    spare_grad[slot] = density_of(v, lefts, SPARE_ROWS)
                    return inner

                lax.fori_loop(0, (count - ROWS + SPARE_ROWS - 1) // SPARE_ROWS, chunk, 0)
                return long_below(v)

            lax.while_loop(lambda v: v >= 0, visit_vert, long_below(jnp.int32(verts)))

        own = [
            cell_of(ix + 1, iy + 1, iz + 1) for ix in range(inner_x) for iy in range(inner_y) for iz in range(inner_z)
        ]
        for c in own:
            grad_lane[c] = jnp.broadcast_to(grad_of(jnp.sum(dens_lane[c], axis=0, keepdims=True)), (8, slots))

        def force_sums(v, k, near_cells, lefts, listed_t, grads):
            width = len(near_cells) * slots
            s = jnp.dot(lefts, right[v, :, k * slots : k * slots + width], preferred_element_type=jnp.float32)
            s = jnp.maximum(s, 0.0)
            fall = jnp.exp2(s)
            both = jnp.concatenate([grads + grad_lane[c, 0:1, :] for c in near_cells], axis=1)
            push = (fall * s) * (fall * (s + PAIR_SHIFT) + both * (s + DENSITY_SHIFT))
            high = push.astype(jnp.bfloat16)
            low = (push - high.astype(jnp.float32)).astype(jnp.bfloat16)
            sums = rows_of(1, 0, listed_t, high) + rows_of(1, 0, listed_t, low)
            return [sums[:, i * slots : (i + 1) * slots] for i in range(len(near_cells))]

        def shares(sums):
            weight = sum(s[ONE_AT : ONE_AT + 1, :] for s in sums)
            whole = sum(sums)
            out = []
            for comp in range(3):
                moment = whole[comp : comp + 1, :] + whole[BLOCK + comp : BLOCK + comp + 1, :]
                moment = (moment + whole[3 * BLOCK + comp : 3 * BLOCK + comp + 1, :]) * (0.5 / SPREAD)
                low_side = sum(sums[k][ONE_AT : ONE_AT + 1, :] for k in range(8) if not (k >> (2 - comp)) & 1)
                out.append(moment + CELL_EDGE * low_side)
            return jnp.concatenate(out + [weight, jnp.zeros((4, slots), jnp.float32)], axis=0)

        def visit_column(n, carry):
            iy = n % inner_y
            ix = n // inner_y
            c = cell_of(ix + 1, iy + 1, 1)
            sums = [[None] * 8 for _ in range(inner_z)]
            for kxy in range(4):
                for vz in range(vert_z):
                    v = vert_of(ix + 1 - (kxy >> 1), iy + 1 - (kxy & 1), vz)
                    sides = [kz for kz in range(2) if 0 <= vz + kz - 1 < inner_z]
                    out = force_sums(
                        v, 2 * kxy + sides[0], [c + vz + kz - 1 for kz in sides], left[v], left_t[v], grad_row[v]
                    )
                    for kz, part in zip(sides, out):
                        sums[vz + kz - 1][2 * kxy + kz] = part
            for iz in range(inner_z):
                totals[c + iz] = shares(sums[iz])
            return carry

        lax.fori_loop(0, inner_x * inner_y, visit_column, 0)

        def spare_force(e, carry):
            v = spare_vert[e]
            none = jnp.zeros((KEPT, slots), jnp.float32)
            for k, c in enumerate(corner_cells(v)):
                sums = force_sums(v, k, [c], spare_left[e], spare_left_t[e], spare_grad[e])[0]
                totals[c] += shares([sums if k == place else none for place in range(8)])
            return carry

        lax.fori_loop(0, spare_count[0], spare_force, 0)

        slot_id = lax.broadcasted_iota(jnp.int32, (1, slots), 1)
        for ix in range(inner_x):
            for iy in range(inner_y):
                c = cell_of(ix + 1, iy + 1, 1)
                n = (ix * inner_y + iy) * inner_z
                for iz in range(inner_z):
                    alive = slot_id < count_ref[n + iz]
                    both = totals[c + iz]
                    for comp in range(3):
                        x = pos_ref[comp, n + iz : n + iz + 1, :]
                        force = FORCE_SCALE * (both[comp : comp + 1, :] - x * both[3:4, :])
                        velocity = vel_ref[comp, n + iz : n + iz + 1, :] + TIME_STEP * force
                        velocity = jnp.where(alive, velocity, 0.0)
                        vel_out[comp, n + iz : n + iz + 1, :] = velocity
                        moved_out[comp, n + iz : n + iz + 1, :] = TIME_STEP * velocity

    own_cells = inner_x * inner_y * inner_z
    vmem = pl.BlockSpec(memory_space=pltpu.VMEM)
    pairs = verts * 8 * ROWS * slots
    return pl.pallas_call(
        kernel,
        out_shape=(jax.ShapeDtypeStruct((3, own_cells, slots), jnp.float32),) * 2,
        in_specs=[vmem] * 3 + [pl.BlockSpec(memory_space=pltpu.SMEM), vmem],
        out_specs=(vmem, vmem),
        scratch_shapes=[
            pltpu.VMEM((3, rows8, slots), jnp.float32),
            pltpu.VMEM((cells * 8, slots), jnp.float32),
            pltpu.VMEM((rows8, slots), jnp.float32),
            pltpu.VMEM((8, slots), jnp.float32),
            pltpu.VMEM((verts, TERMS, lanes), jnp.bfloat16),
            pltpu.VMEM((verts, ROWS, TERMS), jnp.bfloat16),
            pltpu.VMEM((group_size, ROWS, TERMS), jnp.bfloat16),
            pltpu.VMEM((group_size, KEPT, ROWS), jnp.bfloat16),
            pltpu.VMEM((verts, KEPT, ROWS), jnp.bfloat16),
            pltpu.VMEM((verts, ROWS, slots), jnp.float32),
            pltpu.VMEM((cells, 8, slots), jnp.float32),
            pltpu.VMEM((cells, 8, slots), jnp.float32),
            pltpu.VMEM((cells, 8, slots), jnp.float32),
            pltpu.VMEM((spare, SPARE_ROWS, TERMS), jnp.bfloat16),
            pltpu.VMEM((spare, KEPT, SPARE_ROWS), jnp.bfloat16),
            pltpu.VMEM((spare, SPARE_ROWS, slots), jnp.float32),
            pltpu.SMEM((spare,), jnp.int32),
            pltpu.SMEM((1,), jnp.int32),
        ],
        compiler_params=pltpu.CompilerParams(vmem_limit_bytes=36 * 2**20),
        cost_estimate=pl.CostEstimate(flops=40 * pairs, bytes_accessed=4 * 3 * cells * slots, transcendentals=2 * pairs),
        name="block_step",
    )


def body(positions, velocities, counts):
    comps, size_x, size_y, size_z, slots = positions.shape
    own_cells = size_x * size_y * size_z
    slot_index = lax.broadcasted_iota(jnp.int32, counts.shape + (slots,), 3)
    live = slot_index < counts[..., None]
    shown = jnp.where(live[None], positions, FAR)
    ext = with_halo(shown)
    step = block_step((size_x, size_y, size_z), slots)
    velocity, moved = step(
        ext,
        positions.reshape(comps, own_cells, slots),
        velocities.reshape(comps, own_cells, slots),
        counts.reshape(own_cells),
        jnp.asarray(left_matrix(), jnp.bfloat16),
    )
    return velocity.reshape(positions.shape), moved.reshape(positions.shape)


def solution(mesh):
    spec = P(None, *AXES, None)
    return jax.shard_map(
        body,
        mesh=mesh,
        in_specs=(spec, spec, P(*AXES)),
        out_specs=(spec, spec),
        check_vma=False,
    )
```

```python
import math
import jax
import jax.numpy as jnp
import numpy as np
from jax import lax
from jax.experimental import pallas as pl
from jax.experimental.pallas import tpu as pltpu
from jax.sharding import PartitionSpec as P

CELL_EDGE = 11.0
HALF_EDGE = 5.5
REACH = 5.01
CUT_SQ = 25.0
WIDTH_DENSITY = 4.0
WIDTH_PAIR = 2.0
SCALE_DENSITY = 0.4
SCALE_PAIR = 0.3
DENSITY_REF = 1.0
TIME_STEP = 0.5
FAR = 8192.0
AXES = ("gx", "gy", "gz")

TOP_E = CUT_SQ / WIDTH_DENSITY
TOP = TOP_E / math.log(2.0)
SPREAD = math.sqrt(TOP / CUT_SQ)
UNIT = 2.0 * SPREAD
DENSITY_SCALE = SCALE_DENSITY * math.exp(-TOP_E) / TOP**2
PAIR_SHIFT = 4.0 * TOP / CUT_SQ
DENSITY_SHIFT = 8.0 * TOP / CUT_SQ
FORCE_SCALE = -SCALE_PAIR * math.exp(-2.0 * TOP_E) / TOP**2
GRAD_SCALE = SCALE_DENSITY / (2.0 * SCALE_PAIR) * math.exp(TOP_E)

ROWS = 128
SPARE_ROWS = 16
LEFT_PARTS = (0, 0, 1, 0, 2, 1)
RIGHT_PARTS = (0, 1, 0, 2, 0, 1)
BLOCK = 8
TERMS = 6 * BLOCK
KEPT = 4 * BLOCK
NORM_AT = 3
ONE_AT = 4


def neighbour_layers(field, axis, name):
    count = lax.axis_size(name)
    size = field.shape[axis]
    first = lax.slice_in_dim(field, 0, 1, axis=axis)
    last = lax.slice_in_dim(field, size - 1, size, axis=axis)
    if count == 1:
        return last, first
    if count == 2:
        swapped = lax.ppermute(jnp.concatenate([last, first], axis=axis), name, [(0, 1), (1, 0)])
        return lax.slice_in_dim(swapped, 0, 1, axis=axis), lax.slice_in_dim(swapped, 1, 2, axis=axis)
    below = lax.ppermute(last, name, [(d, (d + 1) % count) for d in range(count)])
    above = lax.ppermute(first, name, [(d, (d - 1) % count) for d in range(count)])
    return below, above


def with_halo(field):
    for axis, name in enumerate(AXES, 1):
        below, above = neighbour_layers(field, axis, name)
        field = jnp.concatenate([below, field, above], axis=axis)
    return field


def split_three(value):
    high = value.astype(jnp.bfloat16).astype(jnp.float32)
    rest = value - high
    middle = rest.astype(jnp.bfloat16).astype(jnp.float32)
    return high, middle, rest - middle


def rows_of(contract_a, contract_b, a, b):
    return lax.dot_general(
        a, b, (((contract_a,), (contract_b,)), ((), ())), preferred_element_type=jnp.float32
    )


def left_matrix():
    pick = np.zeros((KEPT, TERMS), np.float32)
    block_of = {0: 0, 1: 1, 2: 3}
    for block, part in enumerate(LEFT_PARTS):
        for comp in range(3):
            pick[block_of[part] * BLOCK + comp, block * BLOCK + comp] = 0.5
    for part, block in ((0, 0), (1, 1), (2, 3)):
        pick[ONE_AT, block * BLOCK + NORM_AT] = 1.0
    for part, block in ((0, 0), (1, 2), (2, 4)):
        pick[block_of[part] * BLOCK + NORM_AT, block * BLOCK + ONE_AT] = 1.0
    return pick.T


def block_step(extent, slots):
    inner_x, inner_y, inner_z = extent
    ext_y, ext_z = inner_y + 2, inner_z + 2
    cells = (inner_x + 2) * ext_y * ext_z
    vert_x, vert_y, vert_z = inner_x + 1, inner_y + 1, inner_z + 1
    verts = vert_x * vert_y * vert_z
    rows8 = verts * 8
    spare = cells * slots // SPARE_ROWS
    lanes = 8 * slots
    group_size = next(size for size in (5, 3, 2, 1) if verts % size == 0)

    def cell_of(cx, cy, cz):
        return (cx * ext_y + cy) * ext_z + cz

    def vert_of(vx, vy, vz):
        return (vx * vert_y + vy) * vert_z + vz

    def corner_cells(v):
        vz = v % vert_z
        vy = (v // vert_z) % vert_y
        vx = v // (vert_z * vert_y)
        return [cell_of(vx + (k >> 2), vy + ((k >> 1) & 1), vz + (k & 1)) for k in range(8)]

    def kernel(ext_ref, pos_ref, vel_ref, count_ref, pick_ref, vel_out, moved_out,
               corner, cell_rows, norms, dest, count_rows, right, left, left_now, listed_now, left_t, grad_row, dens_lane, grad_lane, totals,
               spare_left, spare_left_t, spare_grad, spare_vert, spare_count):
        sub = lax.broadcasted_iota(jnp.int32, (8, slots), 0)
        fill = jnp.where(sub == ONE_AT, 1.0, 0.0)
        for cx in range(inner_x + 2):
            for cy in range(ext_y):
                for cz in range(ext_z):
                    c = cell_of(cx, cy, cz)
                    cell_rows[c * 8 : c * 8 + 8, :] = fill
                    for comp in range(3):
                        cell_rows[c * 8 + comp : c * 8 + comp + 1, :] = ext_ref[comp, cx, cy, cz : cz + 1, :]
        upper = [(sub >> (2 - comp)) & 1 == 1 for comp in range(3)]
        inside = [jnp.where(upper[comp], 1.0, 0.0) for comp in range(3)]
        outside = [1.0 - inside[comp] for comp in range(3)]
        near = []
        for v in range(verts):
            place = (v // (vert_z * vert_y), (v // vert_z) % vert_y, v % vert_z)
            vx, vy, vz = place
            for kxy in range(4):
                for comp in range(3):
                    corner[comp, v * 8 + 2 * kxy : v * 8 + 2 * kxy + 2, :] = ext_ref[
                        comp, vx + kxy // 2, vy + kxy % 2, vz : vz + 2, :
                    ]
            chosen = None
            for comp in range(3):
                above = REACH if place[comp] == extent[comp] else HALF_EDGE
                below = REACH if place[comp] == 0 else HALF_EDGE
                x = corner[comp, v * 8 : v * 8 + 8, :]
                low = x < jnp.where(upper[comp], UNIT * above, UNIT * (CELL_EDGE - below))
                test = jnp.where(low, inside[comp], outside[comp])
                chosen = jnp.where(x < 0.5 * FAR, test, 0.0) if chosen is None else chosen * test
            near.append(chosen)
        near = jnp.concatenate(near, axis=0)
        row_id = lax.broadcasted_iota(jnp.int32, (rows8, slots), 0)
        near_b = near.astype(jnp.bfloat16)
        lane_a = lax.broadcasted_iota(jnp.int32, (slots, slots), 0)
        lane_b = lax.broadcasted_iota(jnp.int32, (slots, slots), 1)
        before = jnp.where(lane_a < lane_b, 1.0, 0.0).astype(jnp.bfloat16)
        prefix = jnp.dot(near_b, before, preferred_element_type=jnp.float32)
        total = jnp.dot(near_b, jnp.ones((slots, slots), jnp.bfloat16), preferred_element_type=jnp.float32)
        earlier = jnp.where((lane_a >> 3 == lane_b >> 3) & (lane_b < lane_a), 1.0, 0.0).astype(jnp.bfloat16)
        offset = []
        for first in range(0, rows8, slots):
            size = min(slots, rows8 - first)
            offset.append(
                jnp.dot(
                    earlier[:size, :size], total[first : first + size, :].astype(jnp.bfloat16),
                    preferred_element_type=jnp.float32,
                )
            )
        offset = jnp.concatenate(offset, axis=0)
        dest[...] = jnp.where(near > 0.5, prefix + offset, -1.0)
        most = jnp.max(offset + total)
        listed_to = offset + total
        dens_lane[...] = jnp.zeros(dens_lane.shape, jnp.float32)

        shifts = []
        for k in range(8):
            shift = jnp.zeros((8, slots), jnp.float32)
            for comp in range(3):
                if not (k >> (2 - comp)) & 1:
                    shift = jnp.where(sub == comp, UNIT * CELL_EDGE, shift)
            shifts.append(shift)
        frames = [jnp.where(upper[comp], 0.0, UNIT * CELL_EDGE) for comp in range(3)]
        for c in range(cells):
            norm = jnp.full((8, slots), 0.5 * TOP, jnp.float32)
            for comp in range(3):
                x = cell_rows[c * 8 + comp : c * 8 + comp + 1, :] - frames[comp]
                norm = norm - 0.25 * (x * x)
            norms[c * 8 : c * 8 + 8, :] = norm

        def terms_of(v):
            packed = []
            for k, c in enumerate(corner_cells(v)):
                x = cell_rows[c * 8 : c * 8 + 8, :] - shifts[k]
                x = jnp.where(sub == NORM_AT, norms[c * 8 + k : c * 8 + k + 1, :], x)
                high, middle, low = split_three(x)
                packed.append([
                    jnp.concatenate([high, part], axis=0).astype(jnp.bfloat16) for part in (middle, low)
                ])
            return packed

        def store_terms(v, packed):
            for k in range(8):
                for pair in range(2):
                    right[v, 16 * pair : 16 * pair + 16, k * slots : (k + 1) * slots] = packed[k][pair]

        def list_of(v, first_row, rows):
            place = (dest[pl.ds(pl.multiple_of(v * 8, 8), 8), :] - first_row).astype(jnp.bfloat16)
            row = lax.broadcasted_iota(jnp.int32, (rows, slots), 0).astype(jnp.float32).astype(jnp.bfloat16)
            one, none = jnp.ones((), jnp.bfloat16), jnp.zeros((), jnp.bfloat16)
            chosen = jnp.concatenate([jnp.where(row == place[k : k + 1, :], one, none) for k in range(8)], axis=1)
            return rows_of(1, 1, right[v], chosen).astype(jnp.bfloat16)

        def lefts_of(listed_t):
            lefts_t = jnp.dot(pick_ref[...], listed_t, preferred_element_type=jnp.float32)
            return lefts_t.T.astype(jnp.bfloat16)

        def meet(lefts, v, first, width):
            kept = right[v, :, first : first + width]
            return jnp.dot(
                lefts, jnp.concatenate([kept, kept[: 2 * BLOCK]], axis=0), preferred_element_type=jnp.float32
            )

        def grad_of(density_sum):
            density = density_sum * DENSITY_SCALE
            return (2.0 * GRAD_SCALE) * (density - (SCALE_DENSITY + DENSITY_REF))

        def distances(v, lefts):
            return [meet(lefts, v, 2 * pair * slots, 2 * slots) for pair in range(4)]

        def density_of(v, pairs, rows, vz=None):
            near_cells = corner_cells(v)
            sums = None
            for pair in range(4):
                for side in range(2):
                    s = jnp.maximum(pairs[pair][:, side * slots : (side + 1) * slots], 0.0)
                    part = jnp.exp2(s) * (s * s)
                    sums = part if sums is None else sums + part
                    if (vz, side) in ((0, 0), (vert_z - 1, 1)):
                        continue
                    dens_lane[near_cells[2 * pair + side]] += jnp.sum(part.reshape(rows // 8, 8, slots), axis=0)
            grad = grad_of(jnp.sum(sums, axis=1, keepdims=True))
            return jnp.broadcast_to(grad, (rows, slots))

        groups = verts // group_size

        def height_of(i):
            return i if group_size == vert_z else None

        def group_of(g):
            return [g * group_size + i for i in range(group_size)]

        def store_lists(g, lists):
            for i, v in enumerate(group_of(g)):
                listed_now[i] = lists[i]
                left_t[v] = lists[i]

        def store_lefts(g, lefts):
            for i, v in enumerate(group_of(g)):
                left_now[i] = lefts[i]
                left[v] = lefts[i]

        def store_grads(g, grads):
            for i, v in enumerate(group_of(g)):
                grad_row[v] = grads[i]

        def visit(g, carry):
            now = [left_now[i] for i in range(group_size)]
            lefts, grads, lists = [], [], []
            pairs = distances(group_of(g)[0], now[0])
            for i, v in enumerate(group_of(g)):
                ahead = distances(group_of(g)[i + 1], now[i + 1]) if i + 1 < group_size else None
                lefts.append(lefts_of(listed_now[i]))
                lists.append(list_of(group_of(g + 2)[i], 0.0, ROWS))
                grads.append(density_of(v, pairs, ROWS, height_of(i)))
                pairs = ahead
            store_grads(g, grads)
            store_lefts(g + 1, lefts)
            store_lists(g + 2, lists)
            return carry

        def visit_last(g, carry):
            store_grads(g, [density_of(v, distances(v, left[v]), ROWS, height_of(i)) for i, v in enumerate(group_of(g))])
            return carry

        for v in range(verts):
            store_terms(v, terms_of(v))
        first = [list_of(v, 0.0, ROWS) for v in group_of(0)]
        store_lists(0, first)
        store_lefts(0, [lefts_of(listed_t) for listed_t in first])
        if groups > 1:
            store_lists(1, [list_of(v, 0.0, ROWS) for v in group_of(1)])
        lax.fori_loop(0, max(groups - 2, 0), visit, 0)
        if groups > 1:
            for i, v in enumerate(group_of(groups - 1)):
                left[v] = lefts_of(listed_now[i])
        lax.fori_loop(max(groups - 2, 0), groups, visit_last, 0)
        spare_count[0] = 0

        @pl.when(most > ROWS)
        def _():
            lane_id = lax.broadcasted_iota(jnp.int32, (rows8, slots), 1)
            ends = jnp.where((row_id & 7 == 7) & (row_id >> 3 == lane_id), listed_to, 0.0)
            count_rows[...] = jnp.broadcast_to(jnp.sum(ends, axis=0, keepdims=True), (8, slots))
            grad_lane[...] = jnp.zeros(grad_lane.shape, jnp.float32)
            vert_id = lax.broadcasted_iota(jnp.int32, (8, slots), 1).astype(jnp.float32)

            def long_below(v):
                wanted = (count_rows[...] > ROWS) & (vert_id < v.astype(jnp.float32))
                return jnp.max(jnp.where(wanted, vert_id, -1.0)).astype(jnp.int32)

            def visit_vert(v):
                count = jnp.max(jnp.where(vert_id == v.astype(jnp.float32), count_rows[...], 0.0)).astype(jnp.int32)

                def chunk(t, inner):
                    slot = spare_count[0]
                    spare_count[0] = slot + 1
                    spare_vert[slot] = v
                    first = ROWS + t * SPARE_ROWS
                    listed_t = list_of(v, first.astype(jnp.float32), SPARE_ROWS)
                    lefts = lefts_of(listed_t)
                    spare_left[slot] = lefts
                    spare_left_t[slot] = listed_t
                    spare_grad[slot] = density_of(v, distances(v, lefts), SPARE_ROWS)
                    return inner

                lax.fori_loop(0, (count - ROWS + SPARE_ROWS - 1) // SPARE_ROWS, chunk, 0)
                return long_below(v)

            lax.while_loop(lambda v: v >= 0, visit_vert, long_below(jnp.int32(verts)))

        own = [
            cell_of(ix + 1, iy + 1, iz + 1) for ix in range(inner_x) for iy in range(inner_y) for iz in range(inner_z)
        ]
        for c in own:
            grad_lane[c] = jnp.broadcast_to(grad_of(jnp.sum(dens_lane[c], axis=0, keepdims=True)), (8, slots))

        def force_sums(near_cells, s, listed_t, grads):
            s = jnp.maximum(s, 0.0)
            fall = jnp.exp2(s)
            both = jnp.concatenate([grads + grad_lane[c, 0:1, :] for c in near_cells], axis=1)
            push = (fall * s) * (fall * (s + PAIR_SHIFT) + both * (s + DENSITY_SHIFT))
            high = push.astype(jnp.bfloat16)
            low = (push - high.astype(jnp.float32)).astype(jnp.bfloat16)
            sums = rows_of(1, 0, listed_t, high) + rows_of(1, 0, listed_t, low)
            return [sums[:, i * slots : (i + 1) * slots] for i in range(len(near_cells))]

        def shares(sums):
            weight = sum(s[ONE_AT : ONE_AT + 1, :] for s in sums)
            whole = sum(sums)
            out = []
            for comp in range(3):
                moment = whole[comp : comp + 1, :] + whole[BLOCK + comp : BLOCK + comp + 1, :]
                moment = (moment + whole[3 * BLOCK + comp : 3 * BLOCK + comp + 1, :]) * (1.0 / UNIT)
                low_side = sum(sums[k][ONE_AT : ONE_AT + 1, :] for k in range(8) if not (k >> (2 - comp)) & 1)
                out.append(moment + CELL_EDGE * low_side)
            return jnp.concatenate(out + [weight, jnp.zeros((4, slots), jnp.float32)], axis=0)

        def visit_column(n, carry):
            iy = n % inner_y
            ix = n // inner_y
            c = cell_of(ix + 1, iy + 1, 1)
            sums = [[None] * 8 for _ in range(inner_z)]
            visits = []
            for kxy in range(4):
                for vz in range(vert_z):
                    sides = [kz for kz in range(2) if 0 <= vz + kz - 1 < inner_z]
                    visits.append((vert_of(ix + 1 - (kxy >> 1), iy + 1 - (kxy & 1), vz), vz, 2 * kxy, sides))

            def met(visit):
                v, vz, k, sides = visit
                return meet(left[v], v, (k + sides[0]) * slots, len(sides) * slots)

            ahead = met(visits[0])
            for at, (v, vz, k, sides) in enumerate(visits):
                s = ahead
                if at + 1 < len(visits):
                    ahead = met(visits[at + 1])
                out = force_sums([c + vz + kz - 1 for kz in sides], s, left_t[v], grad_row[v])
                for kz, part in zip(sides, out):
                    sums[vz + kz - 1][k + kz] = part
            for iz in range(inner_z):
                totals[c + iz] = shares(sums[iz])
            return carry

        lax.fori_loop(0, inner_x * inner_y, visit_column, 0)

        def spare_force(e, carry):
            v = spare_vert[e]
            none = jnp.zeros((KEPT, slots), jnp.float32)
            for k, c in enumerate(corner_cells(v)):
                s = meet(spare_left[e], v, k * slots, slots)
                sums = force_sums([c], s, spare_left_t[e], spare_grad[e])[0]
                totals[c] += shares([sums if k == place else none for place in range(8)])
            return carry

        lax.fori_loop(0, spare_count[0], spare_force, 0)

        slot_id = lax.broadcasted_iota(jnp.int32, (1, slots), 1)
        for ix in range(inner_x):
            for iy in range(inner_y):
                c = cell_of(ix + 1, iy + 1, 1)
                n = (ix * inner_y + iy) * inner_z
                for iz in range(inner_z):
                    alive = slot_id < count_ref[n + iz]
                    both = totals[c + iz]
                    for comp in range(3):
                        x = pos_ref[comp, n + iz : n + iz + 1, :]
                        force = FORCE_SCALE * (both[comp : comp + 1, :] - x * both[3:4, :])
                        velocity = vel_ref[comp, n + iz : n + iz + 1, :] + TIME_STEP * force
                        velocity = jnp.where(alive, velocity, 0.0)
                        vel_out[comp, n + iz : n + iz + 1, :] = velocity
                        moved_out[comp, n + iz : n + iz + 1, :] = TIME_STEP * velocity

    own_cells = inner_x * inner_y * inner_z
    vmem = pl.BlockSpec(memory_space=pltpu.VMEM)
    pairs = verts * 8 * ROWS * slots
    return pl.pallas_call(
        kernel,
        out_shape=(jax.ShapeDtypeStruct((3, own_cells, slots), jnp.float32),) * 2,
        in_specs=[vmem] * 3 + [pl.BlockSpec(memory_space=pltpu.SMEM), vmem],
        out_specs=(vmem, vmem),
        scratch_shapes=[
            pltpu.VMEM((3, rows8, slots), jnp.float32),
            pltpu.VMEM((cells * 8, slots), jnp.float32),
            pltpu.VMEM((cells * 8, slots), jnp.float32),
            pltpu.VMEM((rows8, slots), jnp.float32),
            pltpu.VMEM((8, slots), jnp.float32),
            pltpu.VMEM((verts, KEPT, lanes), jnp.bfloat16),
            pltpu.VMEM((verts, ROWS, TERMS), jnp.bfloat16),
            pltpu.VMEM((group_size, ROWS, TERMS), jnp.bfloat16),
            pltpu.VMEM((group_size, KEPT, ROWS), jnp.bfloat16),
            pltpu.VMEM((verts, KEPT, ROWS), jnp.bfloat16),
            pltpu.VMEM((verts, ROWS, slots), jnp.float32),
            pltpu.VMEM((cells, 8, slots), jnp.float32),
            pltpu.VMEM((cells, 8, slots), jnp.float32),
            pltpu.VMEM((cells, 8, slots), jnp.float32),
            pltpu.VMEM((spare, SPARE_ROWS, TERMS), jnp.bfloat16),
            pltpu.VMEM((spare, KEPT, SPARE_ROWS), jnp.bfloat16),
            pltpu.VMEM((spare, SPARE_ROWS, slots), jnp.float32),
            pltpu.SMEM((spare,), jnp.int32),
            pltpu.SMEM((1,), jnp.int32),
        ],
        compiler_params=pltpu.CompilerParams(vmem_limit_bytes=36 * 2**20),
        cost_estimate=pl.CostEstimate(flops=40 * pairs, bytes_accessed=4 * 3 * cells * slots, transcendentals=2 * pairs),
        name="block_step",
    )


def body(positions, velocities, counts):
    comps, size_x, size_y, size_z, slots = positions.shape
    own_cells = size_x * size_y * size_z
    slot_index = lax.broadcasted_iota(jnp.int32, counts.shape + (slots,), 3)
    live = slot_index < counts[..., None]
    shown = jnp.where(live[None], positions * UNIT, FAR)
    ext = with_halo(shown)
    step = block_step((size_x, size_y, size_z), slots)
    velocity, moved = step(
        ext,
        positions.reshape(comps, own_cells, slots),
        velocities.reshape(comps, own_cells, slots),
        counts.reshape(own_cells),
        jnp.asarray(left_matrix(), jnp.bfloat16),
    )
    return velocity.reshape(positions.shape), moved.reshape(positions.shape)


def solution(mesh):
    spec = P(None, *AXES, None)
    return jax.shard_map(
        body,
        mesh=mesh,
        in_specs=(spec, spec, P(*AXES)),
        out_specs=(spec, spec),
        check_vma=False,
    )
```

```python
import math
import jax
import jax.numpy as jnp
import numpy as np
from jax import lax
from jax.experimental import pallas as pl
from jax.experimental.pallas import tpu as pltpu
from jax.sharding import PartitionSpec as P

CELL_EDGE = 11.0
HALF_EDGE = 5.5
REACH = 5.01
CUT_SQ = 25.0
WIDTH_DENSITY = 4.0
WIDTH_PAIR = 2.0
SCALE_DENSITY = 0.4
SCALE_PAIR = 0.3
DENSITY_REF = 1.0
TIME_STEP = 0.5
FAR = 8192.0
AXES = ("gx", "gy", "gz")

TOP_E = CUT_SQ / WIDTH_DENSITY
TOP = TOP_E / math.log(2.0)
SPREAD = math.sqrt(TOP / CUT_SQ)
UNIT = 2.0 * SPREAD
DENSITY_SCALE = SCALE_DENSITY * math.exp(-TOP_E) / TOP**2
PAIR_SHIFT = 4.0 * TOP / CUT_SQ
DENSITY_SHIFT = 8.0 * TOP / CUT_SQ
FORCE_SCALE = -SCALE_PAIR * math.exp(-2.0 * TOP_E) / TOP**2
GRAD_SCALE = SCALE_DENSITY / (2.0 * SCALE_PAIR) * math.exp(TOP_E)

ROWS = 144
SPARE_ROWS = 16
LISTS_AHEAD = 6
TERMS_AHEAD = 0
LEFT_PARTS = (0, 0, 1, 0, 2, 1)
RIGHT_PARTS = (0, 1, 0, 2, 0, 1)
BLOCK = 8
TERMS = 6 * BLOCK
KEPT = 4 * BLOCK
NORM_AT = 3
ONE_AT = 4


def neighbour_layers(field, axis, name):
    count = lax.axis_size(name)
    size = field.shape[axis]
    first = lax.slice_in_dim(field, 0, 1, axis=axis)
    last = lax.slice_in_dim(field, size - 1, size, axis=axis)
    if count == 1:
        return last, first
    if count == 2:
        swapped = lax.ppermute(jnp.concatenate([last, first], axis=axis), name, [(0, 1), (1, 0)])
        return lax.slice_in_dim(swapped, 0, 1, axis=axis), lax.slice_in_dim(swapped, 1, 2, axis=axis)
    below = lax.ppermute(last, name, [(d, (d + 1) % count) for d in range(count)])
    above = lax.ppermute(first, name, [(d, (d - 1) % count) for d in range(count)])
    return below, above


def with_halo(field):
    for axis, name in enumerate(AXES, 1):
        below, above = neighbour_layers(field, axis, name)
        field = jnp.concatenate([below, field, above], axis=axis)
    return field


def split_three(value):
    high = value.astype(jnp.bfloat16).astype(jnp.float32)
    rest = value - high
    middle = rest.astype(jnp.bfloat16).astype(jnp.float32)
    return high, middle, rest - middle


def rows_of(contract_a, contract_b, a, b):
    return lax.dot_general(
        a, b, (((contract_a,), (contract_b,)), ((), ())), preferred_element_type=jnp.float32
    )


def left_matrix():
    pick = np.zeros((KEPT, TERMS), np.float32)
    block_of = {0: 0, 1: 1, 2: 3}
    for block, part in enumerate(LEFT_PARTS):
        for comp in range(3):
            pick[block_of[part] * BLOCK + comp, block * BLOCK + comp] = 0.5
    for part, block in ((0, 0), (1, 1), (2, 3)):
        pick[ONE_AT, block * BLOCK + NORM_AT] = 1.0
    for part, block in ((0, 0), (1, 2), (2, 4)):
        pick[block_of[part] * BLOCK + NORM_AT, block * BLOCK + ONE_AT] = 1.0
    return pick.T


def block_step(extent, slots):
    inner_x, inner_y, inner_z = extent
    ext_y, ext_z = inner_y + 2, inner_z + 2
    cells = (inner_x + 2) * ext_y * ext_z
    vert_x, vert_y, vert_z = inner_x + 1, inner_y + 1, inner_z + 1
    verts = vert_x * vert_y * vert_z
    rows8 = verts * 8
    spare = cells * slots // SPARE_ROWS
    lanes = 8 * slots

    def cell_of(cx, cy, cz):
        return (cx * ext_y + cy) * ext_z + cz

    def vert_of(vx, vy, vz):
        return (vx * vert_y + vy) * vert_z + vz

    def corner_cells(v):
        vz = v % vert_z
        vy = (v // vert_z) % vert_y
        vx = v // (vert_z * vert_y)
        return [cell_of(vx + (k >> 2), vy + ((k >> 1) & 1), vz + (k & 1)) for k in range(8)]

    def kernel(ext_ref, pos_ref, vel_ref, count_ref, pick_ref, vel_out, moved_out,
               corner, cell_rows, norms, dest, count_rows, right, left, left_t, grad_row, dens_lane, grad_lane, totals,
               spare_left, spare_left_t, spare_grad, spare_vert, spare_count):
        own = [
            cell_of(ix + 1, iy + 1, iz + 1) for ix in range(inner_x) for iy in range(inner_y) for iz in range(inner_z)
        ]
        sub = lax.broadcasted_iota(jnp.int32, (8, slots), 0)
        fill = jnp.where(sub == ONE_AT, 1.0, 0.0)
        for cx in range(inner_x + 2):
            for cy in range(ext_y):
                for cz in range(ext_z):
                    c = cell_of(cx, cy, cz)
                    cell_rows[c * 8 : c * 8 + 8, :] = fill
                    for comp in range(3):
                        cell_rows[c * 8 + comp : c * 8 + comp + 1, :] = ext_ref[comp, cx, cy, cz : cz + 1, :]
        upper = [(sub >> (2 - comp)) & 1 == 1 for comp in range(3)]
        inside = [jnp.where(upper[comp], 1.0, 0.0) for comp in range(3)]
        outside = [1.0 - inside[comp] for comp in range(3)]
        near = []
        for v in range(verts):
            place = (v // (vert_z * vert_y), (v // vert_z) % vert_y, v % vert_z)
            vx, vy, vz = place
            for kxy in range(4):
                for comp in range(3):
                    corner[comp, v * 8 + 2 * kxy : v * 8 + 2 * kxy + 2, :] = ext_ref[
                        comp, vx + kxy // 2, vy + kxy % 2, vz : vz + 2, :
                    ]
            chosen = None
            for comp in range(3):
                above = REACH if place[comp] == extent[comp] else HALF_EDGE
                below = REACH if place[comp] == 0 else HALF_EDGE
                x = corner[comp, v * 8 : v * 8 + 8, :]
                low = x < jnp.where(upper[comp], UNIT * above, UNIT * (CELL_EDGE - below))
                test = jnp.where(low, inside[comp], outside[comp])
                chosen = jnp.where(x < 0.5 * FAR, test, 0.0) if chosen is None else chosen * test
            near.append(chosen)
        near = jnp.concatenate(near, axis=0)
        row_id = lax.broadcasted_iota(jnp.int32, (rows8, slots), 0)
        near_b = near.astype(jnp.bfloat16)
        lane_a = lax.broadcasted_iota(jnp.int32, (slots, slots), 0)
        lane_b = lax.broadcasted_iota(jnp.int32, (slots, slots), 1)
        before = jnp.where(lane_a < lane_b, 1.0, 0.0).astype(jnp.bfloat16)
        prefix = jnp.dot(near_b, before, preferred_element_type=jnp.float32)
        total = jnp.dot(near_b, jnp.ones((slots, slots), jnp.bfloat16), preferred_element_type=jnp.float32)
        earlier = jnp.where((lane_a >> 3 == lane_b >> 3) & (lane_b < lane_a), 1.0, 0.0).astype(jnp.bfloat16)
        offset = []
        for first in range(0, rows8, slots):
            size = min(slots, rows8 - first)
            offset.append(
                jnp.dot(
                    earlier[:size, :size], total[first : first + size, :].astype(jnp.bfloat16),
                    preferred_element_type=jnp.float32,
                )
            )
        offset = jnp.concatenate(offset, axis=0)
        dest[...] = jnp.where(near > 0.5, prefix + offset, -1.0)
        most = jnp.max(offset + total)
        listed_to = offset + total
        dens_lane[...] = jnp.zeros(dens_lane.shape, jnp.float32)

        shifts = []
        for k in range(8):
            shift = jnp.zeros((8, slots), jnp.float32)
            for comp in range(3):
                if not (k >> (2 - comp)) & 1:
                    shift = jnp.where(sub == comp, UNIT * CELL_EDGE, shift)
            shifts.append(shift)
        frames = [jnp.where(upper[comp], 0.0, UNIT * CELL_EDGE) for comp in range(3)]
        for c in range(cells):
            norm = jnp.full((8, slots), 0.5 * TOP, jnp.float32)
            for comp in range(3):
                x = cell_rows[c * 8 + comp : c * 8 + comp + 1, :] - frames[comp]
                norm = norm - 0.25 * (x * x)
            norms[c * 8 : c * 8 + 8, :] = norm

        def terms_of(v):
            packed = []
            for k, c in enumerate(corner_cells(v)):
                x = cell_rows[c * 8 : c * 8 + 8, :] - shifts[k]
                x = jnp.where(sub == NORM_AT, norms[c * 8 + k : c * 8 + k + 1, :], x)
                high, middle, low = split_three(x)
                packed.append([
                    jnp.concatenate([high, part], axis=0).astype(jnp.bfloat16) for part in (middle, low)
                ])
            return packed

        def store_terms(v, packed):
            for k in range(8):
                for pair in range(2):
                    right[v, 16 * pair : 16 * pair + 16, k * slots : (k + 1) * slots] = packed[k][pair]

        def list_of(v, first_row, rows):
            place = (dest[pl.ds(pl.multiple_of(v * 8, 8), 8), :] - first_row).astype(jnp.bfloat16)
            row = lax.broadcasted_iota(jnp.int32, (rows, slots), 0).astype(jnp.float32).astype(jnp.bfloat16)
            one, none = jnp.ones((), jnp.bfloat16), jnp.zeros((), jnp.bfloat16)
            chosen = jnp.concatenate([jnp.where(row == place[k : k + 1, :], one, none) for k in range(8)], axis=1)
            return rows_of(1, 1, right[v], chosen).astype(jnp.bfloat16)

        def lefts_of(listed_t):
            lefts_t = jnp.dot(pick_ref[...], listed_t, preferred_element_type=jnp.float32)
            return lefts_t.T.astype(jnp.bfloat16)

        def meet(lefts, v, first, width):
            kept = right[v, :, first : first + width]
            return jnp.dot(
                lefts, jnp.concatenate([kept, kept[: 2 * BLOCK]], axis=0), preferred_element_type=jnp.float32
            )

        def grad_of(density_sum):
            density = density_sum * DENSITY_SCALE
            return (2.0 * GRAD_SCALE) * (density - (SCALE_DENSITY + DENSITY_REF))

        def distances(v, lefts):
            return [meet(lefts, v, 2 * pair * slots, 2 * slots) for pair in range(4)]

        def density_of(v, pairs, rows):
            near_cells = corner_cells(v)
            sums = None
            for pair in range(4):
                for side in range(2):
                    s = jnp.maximum(pairs[pair][:, side * slots : (side + 1) * slots], 0.0)
                    part = jnp.exp2(s) * (s * s)
                    sums = part if sums is None else sums + part
                    if isinstance(v, int) and near_cells[2 * pair + side] not in own:
                        continue
                    dens_lane[near_cells[2 * pair + side]] += jnp.sum(part.reshape(rows // 8, 8, slots), axis=0)
            grad = grad_of(jnp.sum(sums, axis=1, keepdims=True))
            return jnp.broadcast_to(grad, (rows, slots))

        pairs, held = None, {}
        terms_ahead = TERMS_AHEAD or verts
        for step in range(-terms_ahead, verts):
            if step + terms_ahead < verts:
                store_terms(step + terms_ahead, terms_of(step + terms_ahead))
            ahead = distances(step + 1, left[step + 1]) if 0 <= step + 1 < verts else None
            at = step + LISTS_AHEAD - 2
            if at in held:
                left[at] = lefts_of(held.pop(at))
            at = step + LISTS_AHEAD
            if 0 <= at < verts:
                held[at] = list_of(at, 0.0, ROWS)
                left_t[at] = held[at]
            if step >= 0:
                grad_row[step] = density_of(step, pairs, ROWS)
            pairs = ahead

        spare_count[0] = 0

        @pl.when(most > ROWS)
        def _():
            lane_id = lax.broadcasted_iota(jnp.int32, (rows8, slots), 1)
            ends = jnp.where((row_id & 7 == 7) & (row_id >> 3 == lane_id), listed_to, 0.0)
            count_rows[...] = jnp.broadcast_to(jnp.sum(ends, axis=0, keepdims=True), (8, slots))
            grad_lane[...] = jnp.zeros(grad_lane.shape, jnp.float32)
            vert_id = lax.broadcasted_iota(jnp.int32, (8, slots), 1).astype(jnp.float32)

            def long_below(v):
                wanted = (count_rows[...] > ROWS) & (vert_id < v.astype(jnp.float32))
                return jnp.max(jnp.where(wanted, vert_id, -1.0)).astype(jnp.int32)

            def visit_vert(v):
                count = jnp.max(jnp.where(vert_id == v.astype(jnp.float32), count_rows[...], 0.0)).astype(jnp.int32)

                def chunk(t, inner):
                    slot = spare_count[0]
                    spare_count[0] = slot + 1
                    spare_vert[slot] = v
                    first = ROWS + t * SPARE_ROWS
                    listed_t = list_of(v, first.astype(jnp.float32), SPARE_ROWS)
                    lefts = lefts_of(listed_t)
                    spare_left[slot] = lefts
                    spare_left_t[slot] = listed_t
                    spare_grad[slot] = density_of(v, distances(v, lefts), SPARE_ROWS)
                    return inner

                lax.fori_loop(0, (count - ROWS + SPARE_ROWS - 1) // SPARE_ROWS, chunk, 0)
                return long_below(v)

            lax.while_loop(lambda v: v >= 0, visit_vert, long_below(jnp.int32(verts)))

        for c in own:
            grad_lane[c] = jnp.broadcast_to(grad_of(jnp.sum(dens_lane[c], axis=0, keepdims=True)), (8, slots))

        def force_sums(near_cells, s, listed_t, grads):
            s = jnp.maximum(s, 0.0)
            fall = jnp.exp2(s)
            both = jnp.concatenate([grads + grad_lane[c, 0:1, :] for c in near_cells], axis=1)
            push = (fall * s) * (fall * (s + PAIR_SHIFT) + both * (s + DENSITY_SHIFT))
            high = push.astype(jnp.bfloat16)
            low = (push - high.astype(jnp.float32)).astype(jnp.bfloat16)
            sums = rows_of(1, 0, listed_t, high) + rows_of(1, 0, listed_t, low)
            return [sums[:, i * slots : (i + 1) * slots] for i in range(len(near_cells))]

        def shares(sums):
            weight = sum(s[ONE_AT : ONE_AT + 1, :] for s in sums)
            whole = sum(sums)
            out = []
            for comp in range(3):
                moment = whole[comp : comp + 1, :] + whole[BLOCK + comp : BLOCK + comp + 1, :]
                moment = (moment + whole[3 * BLOCK + comp : 3 * BLOCK + comp + 1, :]) * (1.0 / UNIT)
                low_side = sum(sums[k][ONE_AT : ONE_AT + 1, :] for k in range(8) if not (k >> (2 - comp)) & 1)
                out.append(moment + CELL_EDGE * low_side)
            return jnp.concatenate(out + [weight, jnp.zeros((4, slots), jnp.float32)], axis=0)

        def visit_column(n, carry):
            iy = n % inner_y
            ix = n // inner_y
            c = cell_of(ix + 1, iy + 1, 1)
            sums = [[None] * 8 for _ in range(inner_z)]
            visits = []
            for kxy in range(4):
                for vz in range(vert_z):
                    sides = [kz for kz in range(2) if 0 <= vz + kz - 1 < inner_z]
                    visits.append((vert_of(ix + 1 - (kxy >> 1), iy + 1 - (kxy & 1), vz), vz, 2 * kxy, sides))

            def met(visit):
                v, vz, k, sides = visit
                return meet(left[v], v, (k + sides[0]) * slots, len(sides) * slots)

            ahead = met(visits[0])
            for at, (v, vz, k, sides) in enumerate(visits):
                s = ahead
                if at + 1 < len(visits):
                    ahead = met(visits[at + 1])
                out = force_sums([c + vz + kz - 1 for kz in sides], s, left_t[v], grad_row[v])
                for kz, part in zip(sides, out):
                    sums[vz + kz - 1][k + kz] = part
            for iz in range(inner_z):
                totals[c + iz] = shares(sums[iz])
            return carry

        lax.fori_loop(0, inner_x * inner_y, visit_column, 0)

        def spare_force(e, carry):
            v = spare_vert[e]
            none = jnp.zeros((KEPT, slots), jnp.float32)
            for k, c in enumerate(corner_cells(v)):
                s = meet(spare_left[e], v, k * slots, slots)
                sums = force_sums([c], s, spare_left_t[e], spare_grad[e])[0]
                totals[c] += shares([sums if k == place else none for place in range(8)])
            return carry

        lax.fori_loop(0, spare_count[0], spare_force, 0)

        slot_id = lax.broadcasted_iota(jnp.int32, (1, slots), 1)
        for ix in range(inner_x):
            for iy in range(inner_y):
                c = cell_of(ix + 1, iy + 1, 1)
                n = (ix * inner_y + iy) * inner_z
                for iz in range(inner_z):
                    alive = slot_id < count_ref[n + iz]
                    both = totals[c + iz]
                    for comp in range(3):
                        x = pos_ref[comp, n + iz : n + iz + 1, :]
                        force = FORCE_SCALE * (both[comp : comp + 1, :] - x * both[3:4, :])
                        velocity = vel_ref[comp, n + iz : n + iz + 1, :] + TIME_STEP * force
                        velocity = jnp.where(alive, velocity, 0.0)
                        vel_out[comp, n + iz : n + iz + 1, :] = velocity
                        moved_out[comp, n + iz : n + iz + 1, :] = TIME_STEP * velocity

    own_cells = inner_x * inner_y * inner_z
    vmem = pl.BlockSpec(memory_space=pltpu.VMEM)
    pairs = verts * 8 * ROWS * slots
    return pl.pallas_call(
        kernel,
        out_shape=(jax.ShapeDtypeStruct((3, own_cells, slots), jnp.float32),) * 2,
        in_specs=[vmem] * 3 + [pl.BlockSpec(memory_space=pltpu.SMEM), vmem],
        out_specs=(vmem, vmem),
        scratch_shapes=[
            pltpu.VMEM((3, rows8, slots), jnp.float32),
            pltpu.VMEM((cells * 8, slots), jnp.float32),
            pltpu.VMEM((cells * 8, slots), jnp.float32),
            pltpu.VMEM((rows8, slots), jnp.float32),
            pltpu.VMEM((8, slots), jnp.float32),
            pltpu.VMEM((verts, KEPT, lanes), jnp.bfloat16),
            pltpu.VMEM((verts, ROWS, TERMS), jnp.bfloat16),
            pltpu.VMEM((verts, KEPT, ROWS), jnp.bfloat16),
            pltpu.VMEM((verts, ROWS, slots), jnp.float32),
            pltpu.VMEM((cells, 8, slots), jnp.float32),
            pltpu.VMEM((cells, 8, slots), jnp.float32),
            pltpu.VMEM((cells, 8, slots), jnp.float32),
            pltpu.VMEM((spare, SPARE_ROWS, TERMS), jnp.bfloat16),
            pltpu.VMEM((spare, KEPT, SPARE_ROWS), jnp.bfloat16),
            pltpu.VMEM((spare, SPARE_ROWS, slots), jnp.float32),
            pltpu.SMEM((spare,), jnp.int32),
            pltpu.SMEM((1,), jnp.int32),
        ],
        compiler_params=pltpu.CompilerParams(vmem_limit_bytes=36 * 2**20),
        cost_estimate=pl.CostEstimate(flops=40 * pairs, bytes_accessed=4 * 3 * cells * slots, transcendentals=2 * pairs),
        name="block_step",
    )


def body(positions, velocities, counts):
    comps, size_x, size_y, size_z, slots = positions.shape
    own_cells = size_x * size_y * size_z
    slot_index = lax.broadcasted_iota(jnp.int32, counts.shape + (slots,), 3)
    live = slot_index < counts[..., None]
    shown = jnp.where(live[None], positions * UNIT, FAR)
    ext = with_halo(shown)
    step = block_step((size_x, size_y, size_z), slots)
    velocity, moved = step(
        ext,
        positions.reshape(comps, own_cells, slots),
        velocities.reshape(comps, own_cells, slots),
        counts.reshape(own_cells),
        jnp.asarray(left_matrix(), jnp.bfloat16),
    )
    return velocity.reshape(positions.shape), moved.reshape(positions.shape)


def solution(mesh):
    spec = P(None, *AXES, None)
    return jax.shard_map(
        body,
        mesh=mesh,
        in_specs=(spec, spec, P(*AXES)),
        out_specs=(spec, spec),
        check_vma=False,
    )
```

```python
import math
import jax
import jax.numpy as jnp
import numpy as np
from jax import lax
from jax.experimental import pallas as pl
from jax.experimental.pallas import tpu as pltpu
from jax.sharding import PartitionSpec as P

CELL_EDGE = 11.0
HALF_EDGE = 5.5
REACH = 5.01
CUT_SQ = 25.0
WIDTH_DENSITY = 4.0
WIDTH_PAIR = 2.0
SCALE_DENSITY = 0.4
SCALE_PAIR = 0.3
DENSITY_REF = 1.0
TIME_STEP = 0.5
FAR = 8192.0
AXES = ("gx", "gy", "gz")

TOP_E = CUT_SQ / WIDTH_DENSITY
TOP = TOP_E / math.log(2.0)
SPREAD = math.sqrt(TOP / CUT_SQ)
UNIT = 2.0 * SPREAD
DENSITY_SCALE = SCALE_DENSITY * math.exp(-TOP_E) / TOP**2
PAIR_SHIFT = 4.0 * TOP / CUT_SQ
DENSITY_SHIFT = 8.0 * TOP / CUT_SQ
FORCE_SCALE = -SCALE_PAIR * math.exp(-2.0 * TOP_E) / TOP**2
GRAD_SCALE = SCALE_DENSITY / (2.0 * SCALE_PAIR) * math.exp(TOP_E)

ROWS = 144
SPARE_ROWS = 16
LISTS_AHEAD = 6
TERMS_AHEAD = 0
LEFT_PARTS = (0, 0, 1, 0, 2, 1)
RIGHT_PARTS = (0, 1, 0, 2, 0, 1)
BLOCK = 8
TERMS = 6 * BLOCK
KEPT = 4 * BLOCK
NORM_AT = 3
ONE_AT = 4


def neighbour_layers(field, axis, name):
    count = lax.axis_size(name)
    size = field.shape[axis]
    first = lax.slice_in_dim(field, 0, 1, axis=axis)
    last = lax.slice_in_dim(field, size - 1, size, axis=axis)
    if count == 1:
        return last, first
    if count == 2:
        swapped = lax.ppermute(jnp.concatenate([last, first], axis=axis), name, [(0, 1), (1, 0)])
        return lax.slice_in_dim(swapped, 0, 1, axis=axis), lax.slice_in_dim(swapped, 1, 2, axis=axis)
    below = lax.ppermute(last, name, [(d, (d + 1) % count) for d in range(count)])
    above = lax.ppermute(first, name, [(d, (d - 1) % count) for d in range(count)])
    return below, above


def with_halo(field):
    for axis, name in enumerate(AXES, 1):
        below, above = neighbour_layers(field, axis, name)
        field = jnp.concatenate([below, field, above], axis=axis)
    return field


def split_three(value):
    high = value.astype(jnp.bfloat16).astype(jnp.float32)
    rest = value - high
    middle = rest.astype(jnp.bfloat16).astype(jnp.float32)
    return high, middle, rest - middle


def rows_of(contract_a, contract_b, a, b):
    return lax.dot_general(
        a, b, (((contract_a,), (contract_b,)), ((), ())), preferred_element_type=jnp.float32
    )


def left_matrix():
    pick = np.zeros((KEPT, TERMS), np.float32)
    block_of = {0: 0, 1: 1, 2: 3}
    for block, part in enumerate(LEFT_PARTS):
        for comp in range(3):
            pick[block_of[part] * BLOCK + comp, block * BLOCK + comp] = 0.5
    for part, block in ((0, 0), (1, 1), (2, 3)):
        pick[ONE_AT, block * BLOCK + NORM_AT] = 1.0
    for part, block in ((0, 0), (1, 2), (2, 4)):
        pick[block_of[part] * BLOCK + NORM_AT, block * BLOCK + ONE_AT] = 1.0
    return pick.T


def block_step(extent, slots):
    inner_x, inner_y, inner_z = extent
    ext_y, ext_z = inner_y + 2, inner_z + 2
    cells = (inner_x + 2) * ext_y * ext_z
    vert_x, vert_y, vert_z = inner_x + 1, inner_y + 1, inner_z + 1
    verts = vert_x * vert_y * vert_z
    rows8 = verts * 8
    spare = cells * slots // SPARE_ROWS
    lanes = 8 * slots

    def cell_of(cx, cy, cz):
        return (cx * ext_y + cy) * ext_z + cz

    def vert_of(vx, vy, vz):
        return (vx * vert_y + vy) * vert_z + vz

    def corner_cells(v):
        vz = v % vert_z
        vy = (v // vert_z) % vert_y
        vx = v // (vert_z * vert_y)
        return [cell_of(vx + (k >> 2), vy + ((k >> 1) & 1), vz + (k & 1)) for k in range(8)]

    def kernel(ext_ref, pos_ref, vel_ref, count_ref, pick_ref, vel_out, moved_out,
               corner, cell_rows, norms, dest, count_rows, right, left, left_t, grad_row, dens_lane, grad_lane, totals,
               spare_left, spare_left_t, spare_grad, spare_vert, spare_count):
        own = [
            cell_of(ix + 1, iy + 1, iz + 1) for ix in range(inner_x) for iy in range(inner_y) for iz in range(inner_z)
        ]
        sub = lax.broadcasted_iota(jnp.int32, (8, slots), 0)
        fill = jnp.where(sub == ONE_AT, 1.0, 0.0)
        for cx in range(inner_x + 2):
            for cy in range(ext_y):
                for cz in range(ext_z):
                    c = cell_of(cx, cy, cz)
                    cell_rows[c * 8 : c * 8 + 8, :] = fill
                    for comp in range(3):
                        cell_rows[c * 8 + comp : c * 8 + comp + 1, :] = ext_ref[comp, cx, cy, cz : cz + 1, :]
        upper = [(sub >> (2 - comp)) & 1 == 1 for comp in range(3)]
        inside = [jnp.where(upper[comp], 1.0, 0.0) for comp in range(3)]
        outside = [1.0 - inside[comp] for comp in range(3)]
        near = []
        for v in range(verts):
            place = (v // (vert_z * vert_y), (v // vert_z) % vert_y, v % vert_z)
            vx, vy, vz = place
            for kxy in range(4):
                for comp in range(3):
                    corner[comp, v * 8 + 2 * kxy : v * 8 + 2 * kxy + 2, :] = ext_ref[
                        comp, vx + kxy // 2, vy + kxy % 2, vz : vz + 2, :
                    ]
            chosen = None
            for comp in range(3):
                above = REACH if place[comp] == extent[comp] else HALF_EDGE
                below = REACH if place[comp] == 0 else HALF_EDGE
                x = corner[comp, v * 8 : v * 8 + 8, :]
                low = x < jnp.where(upper[comp], UNIT * above, UNIT * (CELL_EDGE - below))
                test = jnp.where(low, inside[comp], outside[comp])
                chosen = jnp.where(x < 0.5 * FAR, test, 0.0) if chosen is None else chosen * test
            near.append(chosen)
        near = jnp.concatenate(near, axis=0)
        row_id = lax.broadcasted_iota(jnp.int32, (rows8, slots), 0)
        near_b = near.astype(jnp.bfloat16)
        lane_a = lax.broadcasted_iota(jnp.int32, (slots, slots), 0)
        lane_b = lax.broadcasted_iota(jnp.int32, (slots, slots), 1)
        before = jnp.where(lane_a < lane_b, 1.0, 0.0).astype(jnp.bfloat16)
        prefix = jnp.dot(near_b, before, preferred_element_type=jnp.float32)
        total = jnp.dot(near_b, jnp.ones((slots, slots), jnp.bfloat16), preferred_element_type=jnp.float32)
        earlier = jnp.where((lane_a >> 3 == lane_b >> 3) & (lane_b < lane_a), 1.0, 0.0).astype(jnp.bfloat16)
        offset = []
        for first in range(0, rows8, slots):
            size = min(slots, rows8 - first)
            offset.append(
                jnp.dot(
                    earlier[:size, :size], total[first : first + size, :].astype(jnp.bfloat16),
                    preferred_element_type=jnp.float32,
                )
            )
        offset = jnp.concatenate(offset, axis=0)
        dest[...] = jnp.where(near > 0.5, prefix + offset, -1.0)
        most = jnp.max(offset + total)
        listed_to = offset + total
        dens_lane[...] = jnp.zeros(dens_lane.shape, jnp.float32)

        shifts = []
        for k in range(8):
            shift = jnp.zeros((8, slots), jnp.float32)
            for comp in range(3):
                if not (k >> (2 - comp)) & 1:
                    shift = jnp.where(sub == comp, UNIT * CELL_EDGE, shift)
            shifts.append(shift)
        frames = [jnp.where(upper[comp], 0.0, UNIT * CELL_EDGE) for comp in range(3)]
        for c in range(cells):
            norm = jnp.full((8, slots), 0.5 * TOP, jnp.float32)
            for comp in range(3):
                x = cell_rows[c * 8 + comp : c * 8 + comp + 1, :] - frames[comp]
                norm = norm - 0.25 * (x * x)
            norms[c * 8 : c * 8 + 8, :] = norm

        def terms_of(v):
            packed = []
            for k, c in enumerate(corner_cells(v)):
                x = cell_rows[c * 8 : c * 8 + 8, :] - shifts[k]
                x = jnp.where(sub == NORM_AT, norms[c * 8 + k : c * 8 + k + 1, :], x)
                high, middle, low = split_three(x)
                packed.append([
                    jnp.concatenate([high, part], axis=0).astype(jnp.bfloat16) for part in (middle, low)
                ])
            return packed

        def store_terms(v, packed):
            for k in range(8):
                for pair in range(2):
                    right[v, 16 * pair : 16 * pair + 16, k * slots : (k + 1) * slots] = packed[k][pair]

        def list_of(v, first_row, rows):
            place = (dest[pl.ds(pl.multiple_of(v * 8, 8), 8), :] - first_row).astype(jnp.bfloat16)
            row = lax.broadcasted_iota(jnp.int32, (rows, slots), 0).astype(jnp.float32).astype(jnp.bfloat16)
            one, none = jnp.ones((), jnp.bfloat16), jnp.zeros((), jnp.bfloat16)
            chosen = jnp.concatenate([jnp.where(row == place[k : k + 1, :], one, none) for k in range(8)], axis=1)
            return rows_of(1, 1, right[v], chosen).astype(jnp.bfloat16)

        def lefts_of(listed_t):
            lefts_t = jnp.dot(pick_ref[...], listed_t, preferred_element_type=jnp.float32)
            return lefts_t.T.astype(jnp.bfloat16)

        def meet(lefts, v, first, width):
            kept = right[v, :, first : first + width]
            return jnp.dot(
                lefts, jnp.concatenate([kept, kept[: 2 * BLOCK]], axis=0), preferred_element_type=jnp.float32
            )

        def grad_of(density_sum):
            density = density_sum * DENSITY_SCALE
            return (2.0 * GRAD_SCALE) * (density - (SCALE_DENSITY + DENSITY_REF))

        def distances(v, lefts):
            return [meet(lefts, v, 2 * pair * slots, 2 * slots) for pair in range(4)]

        def density_of(v, pairs, rows):
            near_cells = corner_cells(v)
            sums = None
            for pair in range(4):
                for side in range(2):
                    s = jnp.maximum(pairs[pair][:, side * slots : (side + 1) * slots], 0.0)
                    part = jnp.exp2(s) * (s * s)
                    sums = part if sums is None else sums + part
                    if isinstance(v, int) and near_cells[2 * pair + side] not in own:
                        continue
                    dens_lane[near_cells[2 * pair + side]] += jnp.sum(part.reshape(rows // 8, 8, slots), axis=0)
            grad = grad_of(jnp.sum(sums, axis=1, keepdims=True))
            return jnp.broadcast_to(grad, (rows, slots))

        pairs, held = None, {}
        terms_ahead = TERMS_AHEAD or verts
        for step in range(-terms_ahead, verts):
            if step + terms_ahead < verts:
                store_terms(step + terms_ahead, terms_of(step + terms_ahead))
            ahead = distances(step + 1, left[step + 1]) if 0 <= step + 1 < verts else None
            at = step + LISTS_AHEAD - 2
            if at in held:
                left[at] = lefts_of(held.pop(at))
            at = step + LISTS_AHEAD
            if 0 <= at < verts:
                held[at] = list_of(at, 0.0, ROWS)
                left_t[at] = held[at]
            if step >= 0:
                grad_row[step] = density_of(step, pairs, ROWS)
            pairs = ahead

        spare_count[0] = 0

        @pl.when(most > ROWS)
        def _():
            lane_id = lax.broadcasted_iota(jnp.int32, (rows8, slots), 1)
            ends = jnp.where((row_id & 7 == 7) & (row_id >> 3 == lane_id), listed_to, 0.0)
            count_rows[...] = jnp.broadcast_to(jnp.sum(ends, axis=0, keepdims=True), (8, slots))
            grad_lane[...] = jnp.zeros(grad_lane.shape, jnp.float32)
            vert_id = lax.broadcasted_iota(jnp.int32, (8, slots), 1).astype(jnp.float32)

            def long_below(v):
                wanted = (count_rows[...] > ROWS) & (vert_id < v.astype(jnp.float32))
                return jnp.max(jnp.where(wanted, vert_id, -1.0)).astype(jnp.int32)

            def visit_vert(v):
                count = jnp.max(jnp.where(vert_id == v.astype(jnp.float32), count_rows[...], 0.0)).astype(jnp.int32)

                def chunk(t, inner):
                    slot = spare_count[0]
                    spare_count[0] = slot + 1
                    spare_vert[slot] = v
                    first = ROWS + t * SPARE_ROWS
                    listed_t = list_of(v, first.astype(jnp.float32), SPARE_ROWS)
                    lefts = lefts_of(listed_t)
                    spare_left[slot] = lefts
                    spare_left_t[slot] = listed_t
                    spare_grad[slot] = density_of(v, distances(v, lefts), SPARE_ROWS)
                    return inner

                lax.fori_loop(0, (count - ROWS + SPARE_ROWS - 1) // SPARE_ROWS, chunk, 0)
                return long_below(v)

            lax.while_loop(lambda v: v >= 0, visit_vert, long_below(jnp.int32(verts)))

        for c in own:
            grad_lane[c] = jnp.broadcast_to(grad_of(jnp.sum(dens_lane[c], axis=0, keepdims=True)), (8, slots))

        def force_sums(near_cells, s, listed_t, grads):
            s = jnp.maximum(s, 0.0)
            fall = jnp.exp2(s)
            both = jnp.concatenate([grads + grad_lane[c, 0:1, :] for c in near_cells], axis=1)
            push = (fall * s) * (fall * (s + PAIR_SHIFT) + both * (s + DENSITY_SHIFT))
            high = push.astype(jnp.bfloat16)
            low = (push - high.astype(jnp.float32)).astype(jnp.bfloat16)
            sums = rows_of(1, 0, listed_t, high) + rows_of(1, 0, listed_t, low)
            return [sums[:, i * slots : (i + 1) * slots] for i in range(len(near_cells))]

        def shares(sums):
            weight = sum(s[ONE_AT : ONE_AT + 1, :] for s in sums)
            whole = sum(sums)
            out = []
            for comp in range(3):
                moment = whole[comp : comp + 1, :] + whole[BLOCK + comp : BLOCK + comp + 1, :]
                moment = (moment + whole[3 * BLOCK + comp : 3 * BLOCK + comp + 1, :]) * (1.0 / UNIT)
                low_side = sum(sums[k][ONE_AT : ONE_AT + 1, :] for k in range(8) if not (k >> (2 - comp)) & 1)
                out.append(moment + CELL_EDGE * low_side)
            return jnp.concatenate(out + [weight, jnp.zeros((4, slots), jnp.float32)], axis=0)

        def visit_column(n, carry):
            iy = n % inner_y
            ix = n // inner_y
            c = cell_of(ix + 1, iy + 1, 1)
            sums = [[None] * 8 for _ in range(inner_z)]
            visits = []
            for kxy in range(4):
                for vz in range(vert_z):
                    sides = [kz for kz in range(2) if 0 <= vz + kz - 1 < inner_z]
                    visits.append((vert_of(ix + 1 - (kxy >> 1), iy + 1 - (kxy & 1), vz), vz, 2 * kxy, sides))

            def met(visit):
                v, vz, k, sides = visit
                return meet(left[v], v, (k + sides[0]) * slots, len(sides) * slots)

            ahead = met(visits[0])
            for at, (v, vz, k, sides) in enumerate(visits):
                s = ahead
                if at + 1 < len(visits):
                    ahead = met(visits[at + 1])
                out = force_sums([c + vz + kz - 1 for kz in sides], s, left_t[v], grad_row[v])
                for kz, part in zip(sides, out):
                    sums[vz + kz - 1][k + kz] = part
            for iz in range(inner_z):
                totals[c + iz] = shares(sums[iz])
            return carry

        lax.fori_loop(0, inner_x * inner_y, visit_column, 0)

        def spare_force(e, carry):
            v = spare_vert[e]
            none = jnp.zeros((KEPT, slots), jnp.float32)
            for k, c in enumerate(corner_cells(v)):
                s = meet(spare_left[e], v, k * slots, slots)
                sums = force_sums([c], s, spare_left_t[e], spare_grad[e])[0]
                totals[c] += shares([sums if k == place else none for place in range(8)])
            return carry

        lax.fori_loop(0, spare_count[0], spare_force, 0)

        slot_id = lax.broadcasted_iota(jnp.int32, (1, slots), 1)
        for ix in range(inner_x):
            for iy in range(inner_y):
                c = cell_of(ix + 1, iy + 1, 1)
                n = (ix * inner_y + iy) * inner_z
                for iz in range(inner_z):
                    alive = slot_id < count_ref[n + iz]
                    both = totals[c + iz]
                    for comp in range(3):
                        x = pos_ref[comp, n + iz : n + iz + 1, :]
                        force = FORCE_SCALE * (both[comp : comp + 1, :] - x * both[3:4, :])
                        velocity = vel_ref[comp, n + iz : n + iz + 1, :] + TIME_STEP * force
                        velocity = jnp.where(alive, velocity, 0.0)
                        vel_out[comp, n + iz : n + iz + 1, :] = velocity
                        moved_out[comp, n + iz : n + iz + 1, :] = TIME_STEP * velocity

    own_cells = inner_x * inner_y * inner_z
    vmem = pl.BlockSpec(memory_space=pltpu.VMEM)
    pairs = verts * 8 * ROWS * slots
    return pl.pallas_call(
        kernel,
        out_shape=(jax.ShapeDtypeStruct((3, own_cells, slots), jnp.float32),) * 2,
        in_specs=[vmem] * 3 + [pl.BlockSpec(memory_space=pltpu.SMEM), vmem],
        out_specs=(vmem, vmem),
        scratch_shapes=[
            pltpu.VMEM((3, rows8, slots), jnp.float32),
            pltpu.VMEM((cells * 8, slots), jnp.float32),
            pltpu.VMEM((cells * 8, slots), jnp.float32),
            pltpu.VMEM((rows8, slots), jnp.float32),
            pltpu.VMEM((8, slots), jnp.float32),
            pltpu.VMEM((verts, KEPT, lanes), jnp.bfloat16),
            pltpu.VMEM((verts, ROWS, TERMS), jnp.bfloat16),
            pltpu.VMEM((verts, KEPT, ROWS), jnp.bfloat16),
            pltpu.VMEM((verts, ROWS, slots), jnp.float32),
            pltpu.VMEM((cells, 8, slots), jnp.float32),
            pltpu.VMEM((cells, 8, slots), jnp.float32),
            pltpu.VMEM((cells, 8, slots), jnp.float32),
            pltpu.VMEM((spare, SPARE_ROWS, TERMS), jnp.bfloat16),
            pltpu.VMEM((spare, KEPT, SPARE_ROWS), jnp.bfloat16),
            pltpu.VMEM((spare, SPARE_ROWS, slots), jnp.float32),
            pltpu.SMEM((spare,), jnp.int32),
            pltpu.SMEM((1,), jnp.int32),
        ],
        compiler_params=pltpu.CompilerParams(vmem_limit_bytes=36 * 2**20),
        cost_estimate=pl.CostEstimate(flops=40 * pairs, bytes_accessed=4 * 3 * cells * slots, transcendentals=2 * pairs),
        name="block_step",
    )


def body(positions, velocities, counts):
    comps, size_x, size_y, size_z, slots = positions.shape
    own_cells = size_x * size_y * size_z
    slot_index = lax.broadcasted_iota(jnp.int32, positions.shape, 4)
    live = slot_index < lax.broadcast_in_dim(counts, positions.shape, (1, 2, 3))
    shown = jnp.where(live, positions * UNIT, FAR)
    ext = with_halo(shown)
    step = block_step((size_x, size_y, size_z), slots)
    velocity, moved = step(
        ext,
        positions.reshape(comps, own_cells, slots),
        velocities.reshape(comps, own_cells, slots),
        counts.reshape(own_cells),
        jnp.asarray(left_matrix(), jnp.bfloat16),
    )
    return velocity.reshape(positions.shape), moved.reshape(positions.shape)


def solution(mesh):
    spec = P(None, *AXES, None)
    return jax.shard_map(
        body,
        mesh=mesh,
        in_specs=(spec, spec, P(*AXES)),
        out_specs=(spec, spec),
        check_vma=False,
    )
```

```python
import math
import jax
import jax.numpy as jnp
import numpy as np
from jax import lax
from jax.experimental import pallas as pl
from jax.experimental.pallas import tpu as pltpu
from jax.sharding import PartitionSpec as P

CELL_EDGE = 11.0
HALF_EDGE = 5.5
REACH = 5.01
CUT_SQ = 25.0
WIDTH_DENSITY = 4.0
WIDTH_PAIR = 2.0
SCALE_DENSITY = 0.4
SCALE_PAIR = 0.3
DENSITY_REF = 1.0
TIME_STEP = 0.5
FAR = 8192.0
AXES = ("gx", "gy", "gz")

TOP_E = CUT_SQ / WIDTH_DENSITY
TOP = TOP_E / math.log(2.0)
SPREAD = math.sqrt(TOP / CUT_SQ)
UNIT = 2.0 * SPREAD
DENSITY_SCALE = SCALE_DENSITY * math.exp(-TOP_E) / TOP**2
PAIR_SHIFT = 4.0 * TOP / CUT_SQ
DENSITY_SHIFT = 8.0 * TOP / CUT_SQ
FORCE_SCALE = -SCALE_PAIR * math.exp(-2.0 * TOP_E) / TOP**2
GRAD_SCALE = SCALE_DENSITY / (2.0 * SCALE_PAIR) * math.exp(TOP_E)

ROWS = (144, 144, 136, 128)
MOST_ROWS = 144
SPARE_ROWS = 16
LISTS_AHEAD = 6
TERMS_AHEAD = 0
LEFT_PARTS = (0, 0, 1, 0, 2, 1)
RIGHT_PARTS = (0, 1, 0, 2, 0, 1)
BLOCK = 8
TERMS = 6 * BLOCK
KEPT = 4 * BLOCK
NORM_AT = 3
ONE_AT = 4


def neighbour_layers(field, axis, name):
    count = lax.axis_size(name)
    size = field.shape[axis]
    first = lax.slice_in_dim(field, 0, 1, axis=axis)
    last = lax.slice_in_dim(field, size - 1, size, axis=axis)
    if count == 1:
        return last, first
    if count == 2:
        swapped = lax.ppermute(jnp.concatenate([last, first], axis=axis), name, [(0, 1), (1, 0)])
        return lax.slice_in_dim(swapped, 0, 1, axis=axis), lax.slice_in_dim(swapped, 1, 2, axis=axis)
    below = lax.ppermute(last, name, [(d, (d + 1) % count) for d in range(count)])
    above = lax.ppermute(first, name, [(d, (d - 1) % count) for d in range(count)])
    return below, above


def with_halo(field):
    for axis, name in enumerate(AXES, 1):
        below, above = neighbour_layers(field, axis, name)
        field = jnp.concatenate([below, field, above], axis=axis)
    return field


def split_three(value):
    high = value.astype(jnp.bfloat16).astype(jnp.float32)
    rest = value - high
    middle = rest.astype(jnp.bfloat16).astype(jnp.float32)
    return high, middle, rest - middle


def rows_of(contract_a, contract_b, a, b):
    return lax.dot_general(
        a, b, (((contract_a,), (contract_b,)), ((), ())), preferred_element_type=jnp.float32
    )


def left_matrix():
    pick = np.zeros((KEPT, TERMS), np.float32)
    block_of = {0: 0, 1: 1, 2: 3}
    for block, part in enumerate(LEFT_PARTS):
        for comp in range(3):
            pick[block_of[part] * BLOCK + comp, block * BLOCK + comp] = 0.5
    for part, block in ((0, 0), (1, 1), (2, 3)):
        pick[ONE_AT, block * BLOCK + NORM_AT] = 1.0
    for part, block in ((0, 0), (1, 2), (2, 4)):
        pick[block_of[part] * BLOCK + NORM_AT, block * BLOCK + ONE_AT] = 1.0
    return pick.T


def block_step(extent, slots):
    inner_x, inner_y, inner_z = extent
    ext_y, ext_z = inner_y + 2, inner_z + 2
    cells = (inner_x + 2) * ext_y * ext_z
    vert_x, vert_y, vert_z = inner_x + 1, inner_y + 1, inner_z + 1
    verts = vert_x * vert_y * vert_z
    rows8 = verts * 8
    spare = cells * slots // SPARE_ROWS
    lanes = 8 * slots

    def cell_of(cx, cy, cz):
        return (cx * ext_y + cy) * ext_z + cz

    def vert_of(vx, vy, vz):
        return (vx * vert_y + vy) * vert_z + vz

    def boundary_of(v):
        place = (v // (vert_z * vert_y), (v // vert_z) % vert_y, v % vert_z)
        return [place[comp] in (0, extent[comp]) for comp in range(3)]

    def rows_for(v):
        return ROWS[sum(boundary_of(v))]

    def corner_cells(v):
        vz = v % vert_z
        vy = (v // vert_z) % vert_y
        vx = v // (vert_z * vert_y)
        return [cell_of(vx + (k >> 2), vy + ((k >> 1) & 1), vz + (k & 1)) for k in range(8)]

    def kernel(ext_ref, pos_ref, vel_ref, count_ref, pick_ref, vel_out, moved_out,
               corner, cell_rows, norms, dest, count_rows, limit_rows, right, left, left_t, grad_row, dens_lane, grad_lane, totals,
               spare_left, spare_left_t, spare_grad, spare_vert, spare_count):
        own = [
            cell_of(ix + 1, iy + 1, iz + 1) for ix in range(inner_x) for iy in range(inner_y) for iz in range(inner_z)
        ]
        sub = lax.broadcasted_iota(jnp.int32, (8, slots), 0)
        fill = jnp.where(sub == ONE_AT, 1.0, 0.0)
        for cx in range(inner_x + 2):
            for cy in range(ext_y):
                for cz in range(ext_z):
                    c = cell_of(cx, cy, cz)
                    cell_rows[c * 8 : c * 8 + 8, :] = fill
                    for comp in range(3):
                        cell_rows[c * 8 + comp : c * 8 + comp + 1, :] = ext_ref[comp, cx, cy, cz : cz + 1, :]
        upper = [(sub >> (2 - comp)) & 1 == 1 for comp in range(3)]
        inside = [jnp.where(upper[comp], 1.0, 0.0) for comp in range(3)]
        outside = [1.0 - inside[comp] for comp in range(3)]
        near = []
        for v in range(verts):
            place = (v // (vert_z * vert_y), (v // vert_z) % vert_y, v % vert_z)
            vx, vy, vz = place
            for kxy in range(4):
                for comp in range(3):
                    corner[comp, v * 8 + 2 * kxy : v * 8 + 2 * kxy + 2, :] = ext_ref[
                        comp, vx + kxy // 2, vy + kxy % 2, vz : vz + 2, :
                    ]
            chosen, apart = None, 0.0
            for comp in range(3):
                above = REACH if place[comp] == extent[comp] else HALF_EDGE
                below = REACH if place[comp] == 0 else HALF_EDGE
                x = corner[comp, v * 8 : v * 8 + 8, :]
                low = x < jnp.where(upper[comp], UNIT * above, UNIT * (CELL_EDGE - below))
                test = jnp.where(low, inside[comp], outside[comp])
                chosen = jnp.where(x < 0.5 * FAR, test, 0.0) if chosen is None else chosen * test
                if place[comp] == 0:
                    apart = apart + outside[comp] * (UNIT * CELL_EDGE - x) * (UNIT * CELL_EDGE - x)
                elif place[comp] == extent[comp]:
                    apart = apart + inside[comp] * x * x
            if sum(boundary_of(v)) > 1:
                chosen = jnp.where(apart < (UNIT * REACH) ** 2, chosen, 0.0)
            near.append(chosen)
        near = jnp.concatenate(near, axis=0)
        row_id = lax.broadcasted_iota(jnp.int32, (rows8, slots), 0)
        near_b = near.astype(jnp.bfloat16)
        lane_a = lax.broadcasted_iota(jnp.int32, (slots, slots), 0)
        lane_b = lax.broadcasted_iota(jnp.int32, (slots, slots), 1)
        before = jnp.where(lane_a < lane_b, 1.0, 0.0).astype(jnp.bfloat16)
        prefix = jnp.dot(near_b, before, preferred_element_type=jnp.float32)
        total = jnp.dot(near_b, jnp.ones((slots, slots), jnp.bfloat16), preferred_element_type=jnp.float32)
        earlier = jnp.where((lane_a >> 3 == lane_b >> 3) & (lane_b < lane_a), 1.0, 0.0).astype(jnp.bfloat16)
        offset = []
        for first in range(0, rows8, slots):
            size = min(slots, rows8 - first)
            offset.append(
                jnp.dot(
                    earlier[:size, :size], total[first : first + size, :].astype(jnp.bfloat16),
                    preferred_element_type=jnp.float32,
                )
            )
        offset = jnp.concatenate(offset, axis=0)
        dest[...] = jnp.where(near > 0.5, prefix + offset, -1.0)
        limits = jnp.concatenate([jnp.full((8, slots), float(rows_for(v)), jnp.float32) for v in range(verts)], axis=0)
        most = jnp.max(offset + total - limits)
        listed_to = offset + total
        dens_lane[...] = jnp.zeros(dens_lane.shape, jnp.float32)

        shifts = []
        for k in range(8):
            shift = jnp.zeros((8, slots), jnp.float32)
            for comp in range(3):
                if not (k >> (2 - comp)) & 1:
                    shift = jnp.where(sub == comp, UNIT * CELL_EDGE, shift)
            shifts.append(shift)
        frames = [jnp.where(upper[comp], 0.0, UNIT * CELL_EDGE) for comp in range(3)]
        for c in range(cells):
            norm = jnp.full((8, slots), 0.5 * TOP, jnp.float32)
            for comp in range(3):
                x = cell_rows[c * 8 + comp : c * 8 + comp + 1, :] - frames[comp]
                norm = norm - 0.25 * (x * x)
            norms[c * 8 : c * 8 + 8, :] = norm

        def terms_of(v):
            packed = []
            for k, c in enumerate(corner_cells(v)):
                x = cell_rows[c * 8 : c * 8 + 8, :] - shifts[k]
                x = jnp.where(sub == NORM_AT, norms[c * 8 + k : c * 8 + k + 1, :], x)
                high, middle, low = split_three(x)
                packed.append([
                    jnp.concatenate([high, part], axis=0).astype(jnp.bfloat16) for part in (middle, low)
                ])
            return packed

        def store_terms(v, packed):
            for k in range(8):
                for pair in range(2):
                    right[v, 16 * pair : 16 * pair + 16, k * slots : (k + 1) * slots] = packed[k][pair]

        def list_of(v, first_row, rows):
            place = (dest[pl.ds(pl.multiple_of(v * 8, 8), 8), :] - first_row).astype(jnp.bfloat16)
            row = lax.broadcasted_iota(jnp.int32, (rows, slots), 0).astype(jnp.float32).astype(jnp.bfloat16)
            one, none = jnp.ones((), jnp.bfloat16), jnp.zeros((), jnp.bfloat16)
            chosen = jnp.concatenate([jnp.where(row == place[k : k + 1, :], one, none) for k in range(8)], axis=1)
            return rows_of(1, 1, right[v], chosen).astype(jnp.bfloat16)

        def lefts_of(listed_t):
            lefts_t = jnp.dot(pick_ref[...], listed_t, preferred_element_type=jnp.float32)
            return lefts_t.T.astype(jnp.bfloat16)

        def meet(lefts, v, first, width):
            kept = right[v, :, first : first + width]
            return jnp.dot(
                lefts, jnp.concatenate([kept, kept[: 2 * BLOCK]], axis=0), preferred_element_type=jnp.float32
            )

        def grad_of(density_sum):
            density = density_sum * DENSITY_SCALE
            return (2.0 * GRAD_SCALE) * (density - (SCALE_DENSITY + DENSITY_REF))

        def distances(v, lefts):
            return [meet(lefts, v, 2 * pair * slots, 2 * slots) for pair in range(4)]

        def density_of(v, pairs, rows):
            near_cells = corner_cells(v)
            sums = None
            for pair in range(4):
                for side in range(2):
                    s = jnp.maximum(pairs[pair][:, side * slots : (side + 1) * slots], 0.0)
                    part = jnp.exp2(s) * (s * s)
                    sums = part if sums is None else sums + part
                    if isinstance(v, int) and near_cells[2 * pair + side] not in own:
                        continue
                    dens_lane[near_cells[2 * pair + side]] += jnp.sum(part.reshape(rows // 8, 8, slots), axis=0)
            grad = grad_of(jnp.sum(sums, axis=1, keepdims=True))
            return jnp.broadcast_to(grad, (rows, slots))

        for v in range(verts):
            rest = MOST_ROWS - rows_for(v)
            if rest:
                left[v, rows_for(v) :] = jnp.zeros((rest, TERMS), jnp.bfloat16)
                left_t[v, :, rows_for(v) :] = jnp.zeros((KEPT, rest), jnp.bfloat16)
                grad_row[v, rows_for(v) :] = jnp.zeros((rest, slots), jnp.float32)
        pairs, held = None, {}
        terms_ahead = TERMS_AHEAD or verts
        for step in range(-terms_ahead, verts):
            if step + terms_ahead < verts:
                store_terms(step + terms_ahead, terms_of(step + terms_ahead))
            ahead = distances(step + 1, left[step + 1, : rows_for(step + 1)]) if 0 <= step + 1 < verts else None
            at = step + LISTS_AHEAD - 2
            if at in held:
                left[at, : rows_for(at)] = lefts_of(held.pop(at))
            at = step + LISTS_AHEAD
            if 0 <= at < verts:
                rows = rows_for(at)
                held[at] = list_of(at, 0.0, rows)
                left_t[at, :, :rows] = held[at]
            if step >= 0:
                grad_row[step, : rows_for(step)] = density_of(step, pairs, rows_for(step))
            pairs = ahead

        spare_count[0] = 0

        @pl.when(most > 0.0)
        def _():
            lane_id = lax.broadcasted_iota(jnp.int32, (rows8, slots), 1)
            ends = jnp.where((row_id & 7 == 7) & (row_id >> 3 == lane_id), listed_to, 0.0)
            count_rows[...] = jnp.broadcast_to(jnp.sum(ends, axis=0, keepdims=True), (8, slots))
            grad_lane[...] = jnp.zeros(grad_lane.shape, jnp.float32)
            vert_id = lax.broadcasted_iota(jnp.int32, (8, slots), 1).astype(jnp.float32)

            limit = jnp.zeros((8, slots), jnp.float32)
            for v in range(verts):
                limit = jnp.where(vert_id == float(v), float(rows_for(v)), limit)
            limit_rows[...] = limit

            def long_below(v):
                wanted = (count_rows[...] > limit_rows[...]) & (vert_id < v.astype(jnp.float32))
                return jnp.max(jnp.where(wanted, vert_id, -1.0)).astype(jnp.int32)

            def visit_vert(v):
                count = jnp.max(jnp.where(vert_id == v.astype(jnp.float32), count_rows[...], 0.0)).astype(jnp.int32)

                listed = jnp.max(jnp.where(vert_id == v.astype(jnp.float32), limit_rows[...], 0.0)).astype(jnp.int32)

                def chunk(t, inner):
                    slot = spare_count[0]
                    spare_count[0] = slot + 1
                    spare_vert[slot] = v
                    first = listed + t * SPARE_ROWS
                    listed_t = list_of(v, first.astype(jnp.float32), SPARE_ROWS)
                    lefts = lefts_of(listed_t)
                    spare_left[slot] = lefts
                    spare_left_t[slot] = listed_t
                    spare_grad[slot] = density_of(v, distances(v, lefts), SPARE_ROWS)
                    return inner

                lax.fori_loop(0, (count - listed + SPARE_ROWS - 1) // SPARE_ROWS, chunk, 0)
                return long_below(v)

            lax.while_loop(lambda v: v >= 0, visit_vert, long_below(jnp.int32(verts)))

        for c in own:
            grad_lane[c] = jnp.broadcast_to(grad_of(jnp.sum(dens_lane[c], axis=0, keepdims=True)), (8, slots))

        def force_sums(near_cells, s, listed_t, grads):
            s = jnp.maximum(s, 0.0)
            fall = jnp.exp2(s)
            both = jnp.concatenate([grads + grad_lane[c, 0:1, :] for c in near_cells], axis=1)
            push = (fall * s) * (fall * (s + PAIR_SHIFT) + both * (s + DENSITY_SHIFT))
            high = push.astype(jnp.bfloat16)
            low = (push - high.astype(jnp.float32)).astype(jnp.bfloat16)
            sums = rows_of(1, 0, listed_t, high) + rows_of(1, 0, listed_t, low)
            return [sums[:, i * slots : (i + 1) * slots] for i in range(len(near_cells))]

        def shares(sums):
            weight = sum(s[ONE_AT : ONE_AT + 1, :] for s in sums)
            whole = sum(sums)
            out = []
            for comp in range(3):
                moment = whole[comp : comp + 1, :] + whole[BLOCK + comp : BLOCK + comp + 1, :]
                moment = (moment + whole[3 * BLOCK + comp : 3 * BLOCK + comp + 1, :]) * (1.0 / UNIT)
                low_side = sum(sums[k][ONE_AT : ONE_AT + 1, :] for k in range(8) if not (k >> (2 - comp)) & 1)
                out.append(moment + CELL_EDGE * low_side)
            return jnp.concatenate(out + [weight, jnp.zeros((4, slots), jnp.float32)], axis=0)

        def visit_column(n, carry):
            iy = n % inner_y
            ix = n // inner_y
            c = cell_of(ix + 1, iy + 1, 1)
            sums = [[None] * 8 for _ in range(inner_z)]
            visits = []
            for kxy in range(4):
                for vz in range(vert_z):
                    sides = [kz for kz in range(2) if 0 <= vz + kz - 1 < inner_z]
                    visits.append((vert_of(ix + 1 - (kxy >> 1), iy + 1 - (kxy & 1), vz), vz, 2 * kxy, sides))

            def met(visit):
                v, vz, k, sides = visit
                return meet(left[v], v, (k + sides[0]) * slots, len(sides) * slots)

            ahead = met(visits[0])
            for at, (v, vz, k, sides) in enumerate(visits):
                s = ahead
                if at + 1 < len(visits):
                    ahead = met(visits[at + 1])
                out = force_sums([c + vz + kz - 1 for kz in sides], s, left_t[v], grad_row[v])
                for kz, part in zip(sides, out):
                    sums[vz + kz - 1][k + kz] = part
            for iz in range(inner_z):
                totals[c + iz] = shares(sums[iz])
            return carry

        lax.fori_loop(0, inner_x * inner_y, visit_column, 0)

        def spare_force(e, carry):
            v = spare_vert[e]
            none = jnp.zeros((KEPT, slots), jnp.float32)
            for k, c in enumerate(corner_cells(v)):
                s = meet(spare_left[e], v, k * slots, slots)
                sums = force_sums([c], s, spare_left_t[e], spare_grad[e])[0]
                totals[c] += shares([sums if k == place else none for place in range(8)])
            return carry

        lax.fori_loop(0, spare_count[0], spare_force, 0)

        slot_id = lax.broadcasted_iota(jnp.int32, (1, slots), 1)
        for ix in range(inner_x):
            for iy in range(inner_y):
                c = cell_of(ix + 1, iy + 1, 1)
                n = (ix * inner_y + iy) * inner_z
                for iz in range(inner_z):
                    alive = slot_id < count_ref[n + iz]
                    both = totals[c + iz]
                    for comp in range(3):
                        x = pos_ref[comp, n + iz : n + iz + 1, :]
                        force = FORCE_SCALE * (both[comp : comp + 1, :] - x * both[3:4, :])
                        velocity = vel_ref[comp, n + iz : n + iz + 1, :] + TIME_STEP * force
                        velocity = jnp.where(alive, velocity, 0.0)
                        vel_out[comp, n + iz : n + iz + 1, :] = velocity
                        moved_out[comp, n + iz : n + iz + 1, :] = TIME_STEP * velocity

    own_cells = inner_x * inner_y * inner_z
    vmem = pl.BlockSpec(memory_space=pltpu.VMEM)
    pairs = verts * 8 * MOST_ROWS * slots
    return pl.pallas_call(
        kernel,
        out_shape=(jax.ShapeDtypeStruct((3, own_cells, slots), jnp.float32),) * 2,
        in_specs=[vmem] * 3 + [pl.BlockSpec(memory_space=pltpu.SMEM), vmem],
        out_specs=(vmem, vmem),
        scratch_shapes=[
            pltpu.VMEM((3, rows8, slots), jnp.float32),
            pltpu.VMEM((cells * 8, slots), jnp.float32),
            pltpu.VMEM((cells * 8, slots), jnp.float32),
            pltpu.VMEM((rows8, slots), jnp.float32),
            pltpu.VMEM((8, slots), jnp.float32),
            pltpu.VMEM((8, slots), jnp.float32),
            pltpu.VMEM((verts, KEPT, lanes), jnp.bfloat16),
            pltpu.VMEM((verts, MOST_ROWS, TERMS), jnp.bfloat16),
            pltpu.VMEM((verts, KEPT, MOST_ROWS), jnp.bfloat16),
            pltpu.VMEM((verts, MOST_ROWS, slots), jnp.float32),
            pltpu.VMEM((cells, 8, slots), jnp.float32),
            pltpu.VMEM((cells, 8, slots), jnp.float32),
            pltpu.VMEM((cells, 8, slots), jnp.float32),
            pltpu.VMEM((spare, SPARE_ROWS, TERMS), jnp.bfloat16),
            pltpu.VMEM((spare, KEPT, SPARE_ROWS), jnp.bfloat16),
            pltpu.VMEM((spare, SPARE_ROWS, slots), jnp.float32),
            pltpu.SMEM((spare,), jnp.int32),
            pltpu.SMEM((1,), jnp.int32),
        ],
        compiler_params=pltpu.CompilerParams(vmem_limit_bytes=36 * 2**20),
        cost_estimate=pl.CostEstimate(flops=40 * pairs, bytes_accessed=4 * 3 * cells * slots, transcendentals=2 * pairs),
        name="block_step",
    )


def body(positions, velocities, counts):
    comps, size_x, size_y, size_z, slots = positions.shape
    own_cells = size_x * size_y * size_z
    slot_index = lax.broadcasted_iota(jnp.int32, positions.shape, 4)
    live = slot_index < lax.broadcast_in_dim(counts, positions.shape, (1, 2, 3))
    shown = jnp.where(live, positions * UNIT, FAR)
    ext = with_halo(shown)
    step = block_step((size_x, size_y, size_z), slots)
    velocity, moved = step(
        ext,
        positions.reshape(comps, own_cells, slots),
        velocities.reshape(comps, own_cells, slots),
        counts.reshape(own_cells),
        jnp.asarray(left_matrix(), jnp.bfloat16),
    )
    return velocity.reshape(positions.shape), moved.reshape(positions.shape)


def solution(mesh):
    spec = P(None, *AXES, None)
    return jax.shard_map(
        body,
        mesh=mesh,
        in_specs=(spec, spec, P(*AXES)),
        out_specs=(spec, spec),
        check_vma=False,
    )
```
